512 devices in a mesh: section: 64 (over y, z), tp: 8 (over x, core).
Axes of the slice: x: 4, y: 4, z: 16, core: 2. Of those that a mesh axis runs over, the one named last changes fastest.
Arguments:
- preview: bfloat16 [1024, 8192], P('section', 'tp'), may hold values from -6 to 6
- row_owner: int32 [1024], P('section'), may hold values from 0 to 31, never falling along the last dimension, each value on 1 to 128 neighbouring positions
- norm_gain: float32 [8192], P('tp'), may hold values from 0.25 to 1.75
- w_gate: bfloat16 [28672, 8192], P('section', 'tp'), may hold values from -0.0625 to 0.0625
- w_up: bfloat16 [28672, 8192], P('section', 'tp'), may hold values from -0.0625 to 0.0625
- w_down: bfloat16 [28672, 8192], P('section', 'tp'), may hold values from -0.03125 to 0.03125
- score_vec: float32 [8192], P('tp'), may hold values from -0.75 to 0.75
Outputs:
- verified: bfloat16 [1024, 8192], P('section', 'tp')
- scores: float32 [32], replicated
The draws below stay inside these ranges and needn't reach their ends.
Inputs may be any that keep to these rules, and one draw needn't show every extreme that they name: row_owner never falls along the rows; every candidate owns 1 to 128 consecutive rows, some candidate exactly 128.
All inputs are finite; a program needn't handle non-finite values.
Results may differ from the reference program's by a relative error of at most 0.017.
Values may be sent and summed in bfloat16 or wider, within the bound.
A program may use at most 64 MiB of HBM per device.

```python
import math
import jax
import jax.numpy as jnp
import numpy as np
from jax import lax

D = 8192
FF = 28672
CAND = 32
ROWS = 1024
N_TP = 8


def shard_levels(key, extent, shards, low, high):
    def one(position, parts):
        steps = jax.random.uniform(jax.random.fold_in(jax.random.fold_in(key, 6), position), (parts,), jnp.float32, low / len(shards), high / len(shards))
        return jnp.repeat(jnp.exp(steps), extent[position] // parts).reshape((-1,) + (1,) * (len(extent) - position - 1))

    gain = one(*shards[0])
    for cut in shards[1:]:
        gain = gain * one(*cut)
    return gain


def split_up(number_of, total, most, slope):
    loads = [(1 << 20) // math.isqrt(rank ** slope) + 1 for rank in range(2, number_of + 1)]
    rest, given = total - most - (number_of - 1), [1] * (number_of - 1)
    while rest > 0:
        free = [i for i in range(number_of - 1) if given[i] < most]
        pool, budget = sum([loads[i] for i in free]), rest
        for i in free:
            more = min(most - given[i], max(1, budget * loads[i] // pool), rest)
            given[i] = given[i] + more
            rest = rest - more
    return np.array([most] + given)


def ragged(stream_key, amount, total, reach, slope):
    if amount == 2:
        one = jax.random.randint(stream_key, (), max(1, total - reach), min(reach, total - 1) + 1)
        return jnp.stack([one, total - one])
    sizes = jnp.asarray(split_up(amount, total, reach, slope), jnp.int32)
    twos = (amount - 1) // 2
    donor, taker = sizes[1:1 + 2 * twos:2], sizes[2:2 + 2 * twos:2]
    room = jnp.minimum(donor - 1, reach - taker)
    shifted = jax.random.randint(jax.random.fold_in(stream_key, 1), (twos,), 0, 1 << 20) % (room + 1)
    sizes = sizes.at[1:1 + 2 * twos:2].set(donor - shifted).at[2:2 + 2 * twos:2].set(taker + shifted)
    return sizes[jax.random.permutation(jax.random.fold_in(stream_key, 2), amount)]


def gaussian(stream_key, shape, scale, limit, pieces=(), held_as=jnp.bfloat16):
    level = shard_levels(stream_key, shape, pieces, -0.22, 0.18) if pieces else 1.0
    result = jax.random.normal(stream_key, shape, jnp.float32) * scale * level
    return jnp.minimum(jnp.maximum(result, -limit), limit).astype(held_as)


def setup_inputs(seed: int = 0) -> dict:
    splits = jax.random.split(jax.random.key(seed), 8)
    preview = gaussian(splits[0], (ROWS, D), 1.0, 6.0, ((0, 64), (1, 8)))
    row_owner = jnp.searchsorted(jnp.cumsum(ragged(splits[1], CAND, ROWS, ROWS // 8, 2)), jnp.arange(ROWS), side="right").astype(jnp.int32)
    norm_gain = jnp.clip(1.0 + 0.15 * jax.random.normal(splits[2], (D,), jnp.float32), 0.25, 1.75)
    w_gate = gaussian(splits[3], (FF, D), D ** -0.5, 0.0625, ((0, 64), (1, 8)))
    w_up = gaussian(splits[4], (FF, D), D ** -0.5, 0.0625, ((0, 64), (1, 8)))
    w_down = gaussian(splits[5], (FF, D), FF ** -0.5, 0.03125, ((0, 64), (1, 8)))
    score_vec = gaussian(splits[6], (D,), 64 ** -0.5, 0.75, ((0, 8),), jnp.float32)
    return {"preview": preview, "row_owner": row_owner, "norm_gain": norm_gain, "w_gate": w_gate, "w_up": w_up, "w_down": w_down, "score_vec": score_vec}


def reference(preview, row_owner, norm_gain, w_gate, w_up, w_down, score_vec):
    resid = preview.astype(jnp.float32)
    mean_sq = lax.optimization_barrier(jnp.mean(resid * resid, axis=1, keepdims=True))
    normed = (resid * lax.rsqrt(mean_sq + 1e-05) * norm_gain[None, :]).astype(jnp.bfloat16)
    width = D // N_TP
    dims = (((1,), (1,)), ((), ()))
    gate = jnp.zeros((ROWS, FF), jnp.float32)
    up = jnp.zeros((ROWS, FF), jnp.float32)
    for block in range(N_TP):
        lo = block * width
        part_x = normed[:, lo:lo + width]
        gate = gate + lax.dot_general(part_x, w_gate[:, lo:lo + width], dims, preferred_element_type=jnp.float32).astype(jnp.bfloat16).astype(jnp.float32)
        up = up + lax.dot_general(part_x, w_up[:, lo:lo + width], dims, preferred_element_type=jnp.float32).astype(jnp.bfloat16).astype(jnp.float32)
    hidden = (jax.nn.silu(gate) * up).astype(jnp.bfloat16)
    verified = (resid + jnp.dot(hidden, w_down, preferred_element_type=jnp.float32)).astype(jnp.bfloat16)
    row_score = jnp.dot(verified.astype(jnp.float32), score_vec, precision=lax.Precision.HIGHEST)
    member = (row_owner[None, :] == jnp.arange(CAND, dtype=jnp.int32)[:, None]).astype(jnp.float32)
    totals = jnp.dot(member, row_score, precision=lax.Precision.HIGHEST)
    counts = lax.optimization_barrier(jnp.sum(member, axis=1))
    return (verified, totals / counts)
```

```python
import functools

import jax
import jax.numpy as jnp
from jax import lax
from jax.experimental import pallas as pl
from jax.experimental.pallas import tpu as pltpu
from jax.sharding import PartitionSpec as P

CAND = 32
NY = 4
NX = 4
EPS = 1e-05
BF = jnp.bfloat16
F32 = jnp.float32


class Plan:
    def __init__(self, nz, rows, feats, hidden, groups):
        self.nz, self.hz = nz, nz // 2
        self.rows, self.feats, self.hidden = rows, feats, hidden
        self.ng, self.q = groups, nz // groups
        self.half = self.q // 2 * NY * rows
        self.blk = self.half // NX
        self.hpad = -(-hidden // 128) * 128
        self.full = hidden // 128 * 128
        self.rest = hidden - self.full
        tiles = feats // 128
        self.wa = max(1, (tiles * 3) // 8) * 128
        self.wb = feats - self.wa
        self.wc = max(1, self.wb // 128 // 2 + (self.wb // 128) % 2) * 128
        if self.wc >= self.wb:
            self.wc = self.wb


def kernel(pn, prev_ref, owner_ref, gain_ref, wg_ref, wu_ref, wd_ref, sv_ref, out_ref, score_ref,
           x, wgu, wd, nrm, gus, guo, rc, rx1, rx2, gux, hid, pt, rza, rzb, ry1, ry2, rya, sc, lsem, ssem, rsem):
    nz, hz = pn.nz, pn.hz
    wa, wb, wc = pn.wa, pn.wb, pn.wc
    A, B = pl.ds(0, wa), pl.ds(wa, wb)
    B1, B2 = pl.ds(wa, wc), pl.ds(wa + wc, wb - wc)
    s, t = lax.axis_index("section"), lax.axis_index("tp")
    yy, zz = s // nz, s % nz
    xx, cc = t // 2, t % 2

    def dev(dx=0, dy=0, dz=0, other=False):
        sec = ((yy + dy) % NY) * nz + (zz + dz) % nz
        core = 1 - cc if other else cc
        return (sec, ((xx + dx) % NX) * 2 + core)

    count = [0]
    flying = []

    def send(src, dst, to):
        i = count[0]
        count[0] += 1
        copy = pltpu.make_async_remote_copy(
            src_ref=src, dst_ref=dst, send_sem=ssem.at[i], recv_sem=rsem.at[i],
            device_id=to, device_id_type=pl.DeviceIdType.MESH)
        copy.start()
        flying.append(copy)
        return copy

    full, rest = pn.full, pn.rest
    loads = []

    def load(src, dst):
        copy = pltpu.make_async_copy(src, dst, lsem.at[len(loads)])
        copy.start()
        loads.append(copy)

    if full:
        load(wg_ref.at[pl.ds(0, full)], wgu.at[pl.ds(0, full)])
        load(wu_ref.at[pl.ds(0, full)], wgu.at[pl.ds(full, full)])
    if rest:
        load(wg_ref.at[pl.ds(full, rest)], wgu.at[pl.ds(2 * full, rest)])
        load(wu_ref.at[pl.ds(full, rest)], wgu.at[pl.ds(2 * full + rest, rest)])
    load(wd_ref, wd.at[pl.ds(0, pn.hidden)])
    if rest:
        wd[pl.ds(pn.hidden, pn.hpad - pn.hidden), :] = jnp.zeros((pn.hpad - pn.hidden, pn.feats), BF)

    tp_peers = [dev(dx=dx, other=o) for dx in range(NX) for o in (False, True) if (dx, o) != (0, False)]
    y_peers = [dev(dy=dy) for dy in range(1, NY)]
    z_peers = [dev(dz=dz) for dz in range(1, nz)]
    barrier = pltpu.get_barrier_semaphore()
    for peer in tp_peers + y_peers + z_peers:
        pl.semaphore_signal(barrier, inc=1, device_id=peer, device_id_type=pl.DeviceIdType.MESH)
    pl.semaphore_wait(barrier, len(tp_peers + y_peers + z_peers))

    own = prev_ref[...].astype(F32)
    sq = jnp.sum(own * own, axis=1, keepdims=True)
    nrm[0] = jnp.broadcast_to(sq, (pn.rows, 128))
    copies = [send(nrm.at[0], nrm.at[i + 1], peer) for i, peer in enumerate(tp_peers)]
    for c in copies:
        c.wait_recv()
    tot = nrm[0]
    for i in range(len(tp_peers)):
        tot = tot + nrm[i + 1]
    rs = lax.rsqrt(tot[:, 0:1] / (pn.feats * NX * 2) + EPS)
    x[0, 0] = (own * rs * gain_ref[...]).astype(BF)

    def pair(k):
        if k == 0:
            return [0]
        return [nz - 1] if k == hz else [2 * k - 1, 2 * k]

    def pslice(k):
        p = pair(k)
        return pl.ds(p[0], len(p))

    def gather():
        za, zb, y1, y2 = {}, {}, {}, {}

        def step_b(k):
            lo, hi = max(2 * k - 3, 0), 2 * k - 2
            if k < hz:
                zb[k] = [send(x.at[lo, 0, :, B], x.at[2 * k - 1, 0, :, B], dev(dz=1)),
                         send(x.at[hi, 0, :, B], x.at[2 * k, 0, :, B], dev(dz=-1))]
            else:
                zb[k] = [send(x.at[lo, 0, :, B1], x.at[nz - 1, 0, :, B1], dev(dz=1))]
                if wc < wb:
                    zb[k].append(send(x.at[hi, 0, :, B2], x.at[nz - 1, 0, :, B2], dev(dz=-1)))

        def step_a(k):
            lo, hi = max(2 * k - 3, 0), 2 * k - 2
            if k < hz:
                za[k] = [send(x.at[lo, :, :, A], x.at[2 * k - 1, :, :, A], dev(dz=1)),
                         send(x.at[hi, :, :, A], x.at[2 * k, :, :, A], dev(dz=-1))]
            else:
                za[k] = [send(x.at[lo, pl.ds(0, 2), :, A], x.at[nz - 1, pl.ds(0, 2), :, A], dev(dz=1)),
                         send(x.at[hi, pl.ds(2, 2), :, A], x.at[nz - 1, pl.ds(2, 2), :, A], dev(dz=-1))]

        def step_y1(k):
            y1[k] = [send(x.at[pslice(k), 0, :, B], x.at[pslice(k), 1, :, B], dev(dy=1)),
                     send(x.at[pslice(k), 0, :, B], x.at[pslice(k), 2, :, B], dev(dy=-1))]

        def step_y2(k):
            for c in y1[k]:
                c.wait_recv()
            y2[k] = []
            for q in pair(k):
                j, dy = (1, 1) if q % 2 else (2, -1)
                y2[k].append(send(x.at[q, j, :, B], x.at[q, 3, :, B], dev(dy=dy)))

        def finish_y2(k):
            for c in y2[k]:
                c.wait_recv()

        first = [send(x.at[0, 0, :, A], x.at[0, 1, :, A], dev(dy=1)),
                 send(x.at[0, 0, :, A], x.at[0, 2, :, A], dev(dy=-1)),
                 send(x.at[0, 0, :, A], x.at[0, 3, :, A], dev(dy=2))]
        step_b(1)
        step_y1(0)
        for c in first:
            c.wait_recv()
        step_a(1)
        for k in range(1, hz + 3):
            if k <= hz:
                for c in zb[k]:
                    c.wait_recv()
                if k < hz:
                    step_b(k + 1)
                step_y1(k)
                for c in za[k]:
                    c.wait_recv()
                if k < hz:
                    step_a(k + 1)
            if k - 1 <= hz:
                step_y2(k - 1)
            if k >= 2:
                finish_y2(k - 2)
                yield k - 2

    dims = (((1,), (1,)), ((), ()))
    hq = pn.q // 2
    half, blk = pn.half, pn.blk

    def product(q0):
        rows = x[pl.ds(q0, hq)].reshape(half, pn.feats)
        return lax.dot_general(rows, wgu[...], dims, preferred_element_type=F32)

    def group(g):
        other, mine = g * pn.q + (1 - cc) * hq, g * pn.q + cc * hq
        gus[g] = product(other).astype(BF)
        c1 = send(gus.at[g], rc.at[g], dev(other=True))
        guo[g] = product(mine)
        yield
        c1.wait_recv()
        guo[g] = guo[g] + rc[g].astype(F32)

        def at(dx, start=0):
            return pl.multiple_of(((xx + dx) % NX) * blk, blk) + start

        hb = blk // 2
        gux[g, 2] = guo[g, pl.ds(at(2), blk)].astype(BF)
        x1 = [send(gux.at[g, 2, pl.ds(0, hb)], rx1.at[g, 0], dev(dx=1)),
              send(gux.at[g, 2, pl.ds(hb, hb)], rx1.at[g, 1], dev(dx=-1))]
        yield
        for c in x1:
            c.wait_recv()
        gux[g, 0, pl.ds(0, hb)] = (guo[g, pl.ds(at(1), hb)] + rx1[g, 0].astype(F32)).astype(BF)
        gux[g, 0, pl.ds(hb, hb)] = guo[g, pl.ds(at(1, hb), hb)].astype(BF)
        gux[g, 1, pl.ds(0, hb)] = guo[g, pl.ds(at(-1), hb)].astype(BF)
        gux[g, 1, pl.ds(hb, hb)] = (guo[g, pl.ds(at(-1, hb), hb)] + rx1[g, 1].astype(F32)).astype(BF)
        x2 = [send(gux.at[g, 0], rx2.at[g, 0], dev(dx=1)),
              send(gux.at[g, 1], rx2.at[g, 1], dev(dx=-1))]
        yield
        for c in x2:
            c.wait_recv()
        gu = guo[g, pl.ds(at(0), blk)] + rx2[g, 0].astype(F32) + rx2[g, 1].astype(F32)

        def act(gate, up):
            return (gate / (1.0 + jnp.exp(-gate)) * up).astype(BF)

        if full:
            hid[g, cc, xx, :, pl.ds(0, full)] = act(gu[:, 0:full], gu[:, full:2 * full])
        if rest:
            last = gu[:, 2 * full:]
            lane = lax.broadcasted_iota(jnp.int32, last.shape, 1)
            value = act(last, pltpu.roll(last, 128 - rest, 1))
            hid[g, cc, xx, :, pl.ds(full, 128)] = jnp.where(lane < rest, value, jnp.zeros_like(value))
        own_h = hid.at[g, cc, xx]
        h1 = [send(own_h, own_h, dev(dx=1)), send(own_h, own_h, dev(dx=-1))]
        yield
        for c in h1:
            c.wait_recv()
        left = hid.at[g, cc, (xx + NX - 1) % NX, pl.ds(0, hb)]
        right = hid.at[g, cc, (xx + 1) % NX, pl.ds(hb, hb)]
        h2 = [send(left, left, dev(dx=1)), send(right, right, dev(dx=-1))]
        yield
        for c in h2:
            c.wait_recv()
        c2 = send(hid.at[g, cc], hid.at[g, cc], dev(other=True))
        yield
        c2.wait_recv()
        rows = hid[g].reshape(2 * half, pn.hpad)
        down = jnp.dot(rows, wd[...], preferred_element_type=F32)
        pt[pl.ds(g * pn.q, pn.q)] = down.astype(BF).reshape(pn.q, NY, pn.rows, pn.feats)

    waiting = list(range(pn.ng))
    active = []
    loaded = [False]

    def advance():
        for gen in list(active):
            try:
                next(gen)
            except StopIteration:
                active.remove(gen)

    for done in gather():
        advance()
        if waiting and done >= ((waiting[0] + 1) * pn.q) // 2:
            if not loaded[0]:
                for c in loads:
                    c.wait()
                loaded[0] = True
            gen = group(waiting.pop(0))
            next(gen)
            active.append(gen)
    while active:
        advance()

    def add(dst, *terms):
        v = dst[...].astype(F32)
        for term in terms:
            v = v + term.astype(F32)
        dst[...] = v.astype(BF)

    za, zb, y1, y2 = {}, {}, {}, {}

    def rs_a(m):
        if m == hz:
            q = nz - 1
            za[m] = [send(pt.at[q, pl.ds(0, 2), :, A], rza.at[m - 1, 0, pl.ds(0, 2)], dev(dz=1)),
                     send(pt.at[q, pl.ds(2, 2), :, A], rza.at[m - 1, 1, pl.ds(2, 2)], dev(dz=-1))]
            return
        for c in za[m + 1]:
            c.wait_recv()
        for d, q in ((0, 2 * m), (1, 2 * m - 1)):
            js = pl.ds(0, NY) if m + 1 < hz else pl.ds(2 * d, 2)
            add(pt.at[q, js, :, A], rza[m, d, js])
        za[m] = [send(pt.at[2 * m, :, :, A], rza.at[m - 1, 0], dev(dz=1)),
                 send(pt.at[2 * m - 1, :, :, A], rza.at[m - 1, 1], dev(dz=-1))]

    def part(m, d):
        if m < hz:
            return B, pl.ds(0, wb)
        return (B1, pl.ds(0, wc)) if d == 0 else (B2, pl.ds(wc, wb - wc))

    def rs_b(m):
        if m < hz:
            for c in zb[m + 1]:
                c.wait_recv()
            for d, q in ((0, 2 * m), (1, 2 * m - 1)):
                cols, rcols = part(m + 1, d)
                if cols.size:
                    add(pt.at[q, 0, :, cols], rzb[m, d, :, rcols])
        zb[m] = []
        for d, dz in ((0, 1), (1, -1)):
            q = nz - 1 if m == hz else 2 * m - d
            cols, rcols = part(m, d)
            if cols.size:
                zb[m].append(send(pt.at[q, 0, :, cols], rzb.at[m - 1, d, :, rcols], dev(dz=dz)))

    def rs_y1(m):
        y1[m] = [send(pt.at[q, 3, :, B], ry1.at[q], dev(dy=1 if q % 2 else -1)) for q in pair(m)]

    def rs_y2(m):
        for c in y1[m]:
            c.wait_recv()
        for q in pair(m):
            add(pt.at[q, 2 if q % 2 else 1, :, B], ry1[q])
        y2[m] = [send(pt.at[pslice(m), 2, :, B], ry2.at[0, pslice(m)], dev(dy=1)),
                 send(pt.at[pslice(m), 1, :, B], ry2.at[1, pslice(m)], dev(dy=-1))]

    def rs_y3(m):
        for c in y2[m]:
            c.wait_recv()
        for q in pair(m):
            add(pt.at[q, 0, :, B], ry2[0, q], ry2[1, q])

    fin = []
    for i in range(hz + 3):
        m = hz - i
        if m >= 0:
            rs_y1(m)
        if m >= 1:
            rs_a(m)
        if m == 0:
            for c in za[1]:
                c.wait_recv()
            add(pt.at[0, :, :, A], rza[0, 0], rza[0, 1])
            fin = [send(pt.at[0, 1, :, A], rya.at[0], dev(dy=-1)),
                   send(pt.at[0, 2, :, A], rya.at[1], dev(dy=1)),
                   send(pt.at[0, 3, :, A], rya.at[2], dev(dy=2))]
        if 0 <= m + 1 <= hz:
            rs_y2(m + 1)
        if 0 <= m + 2 <= hz:
            rs_y3(m + 2)
            if m + 2 >= 1:
                rs_b(m + 2)
    for c in fin:
        c.wait_recv()
    va = pt[0, 0, :, A].astype(F32)
    for i in range(3):
        va = va + rya[i].astype(F32)
    va = (va + prev_ref[:, A].astype(F32)).astype(BF)
    out_ref[:, A] = va
    for c in zb[1]:
        c.wait_recv()
    vb = pt[0, 0, :, B].astype(F32) + rzb[0, 0].astype(F32) + rzb[0, 1].astype(F32)
    vb = (vb + prev_ref[:, B].astype(F32)).astype(BF)
    out_ref[:, B] = vb

    row = (jnp.sum(va.astype(F32) * sv_ref[:, A], axis=1, keepdims=True)
           + jnp.sum(vb.astype(F32) * sv_ref[:, B], axis=1, keepdims=True))
    lane = lax.broadcasted_iota(jnp.int32, (1, 128), 1)
    total = jnp.zeros((1, 128), F32)
    number = jnp.zeros((1, 128), F32)
    for r in range(pn.rows):
        hit = lane == owner_ref[r]
        total = total + jnp.where(hit, row[r:r + 1, :], 0.0)
        number = number + jnp.where(hit, 1.0, 0.0)
    sub = lax.broadcasted_iota(jnp.int32, (8, 128), 0)
    acc = jnp.where(sub == 0, total, jnp.where(sub == 1, number, 0.0))
    base = 0
    for peers in (tp_peers, y_peers, z_peers):
        sc[base] = acc
        copies = [send(sc.at[base], sc.at[base + 1 + i], peer) for i, peer in enumerate(peers)]
        for i, c in enumerate(copies):
            c.wait_recv()
            acc = acc + sc[base + 1 + i]
        base += 1 + len(peers)
    score_ref[...] = acc[0:1, :] / jnp.maximum(acc[1:2, :] / (NX * 2), 1e-30)
    for c in flying:
        c.wait_send()


def shards(nz, groups, preview, row_owner, norm_gain, w_gate, w_up, w_down, score_vec):
    rows, feats = preview.shape
    hidden = w_gate.shape[0]
    pn = Plan(nz, rows, feats, hidden, groups)
    ng, half, blk = pn.ng, pn.half, pn.blk
    width = 2 * hidden
    sems = 600
    vmem = pl.BlockSpec(memory_space=pltpu.VMEM)
    hbm = pl.BlockSpec(memory_space=pl.ANY)
    verified, scores = pl.pallas_call(
        functools.partial(kernel, pn),
        out_shape=(jax.ShapeDtypeStruct((rows, feats), BF), jax.ShapeDtypeStruct((1, 128), F32)),
        in_specs=[vmem, pl.BlockSpec(memory_space=pltpu.SMEM), vmem, hbm, hbm, hbm, vmem],
        out_specs=(vmem, vmem),
        scratch_shapes=[
            pltpu.VMEM((nz, NY, rows, feats), BF),
            pltpu.VMEM((width, feats), BF),
            pltpu.VMEM((pn.hpad, feats), BF),
            pltpu.VMEM((2 * NX, rows, 128), F32),
            pltpu.VMEM((ng, half, width), BF),
            pltpu.VMEM((ng, half, width), F32),
            pltpu.VMEM((ng, half, width), BF),
            pltpu.VMEM((ng, 2, blk // 2, width), BF),
            pltpu.VMEM((ng, 2, blk, width), BF),
            pltpu.VMEM((ng, 3, blk, width), BF),
            pltpu.VMEM((ng, 2, NX, blk, pn.hpad), BF),
            pltpu.VMEM((nz, NY, rows, feats), BF),
            pltpu.VMEM((pn.hz, 2, NY, rows, pn.wa), BF),
            pltpu.VMEM((pn.hz, 2, rows, pn.wb), BF),
            pltpu.VMEM((nz, rows, pn.wb), BF),
            pltpu.VMEM((2, nz, rows, pn.wb), BF),
            pltpu.VMEM((3, rows, pn.wa), BF),
            pltpu.VMEM((2 * NX + NY + nz, 8, 128), F32),
            pltpu.SemaphoreType.DMA((5,)),
            pltpu.SemaphoreType.DMA((sems,)),
            pltpu.SemaphoreType.DMA((sems,)),
        ],
        compiler_params=pltpu.CompilerParams(
            collective_id=0, has_side_effects=True, vmem_limit_bytes=56 << 20),
    )(preview, row_owner, norm_gain[None, :], w_gate, w_up, w_down, score_vec[None, :])
    return verified, scores[0, :CAND]


def solution(mesh):
    placed = (
        P("section", "tp"),
        P("section"),
        P("tp"),
        P("section", "tp"),
        P("section", "tp"),
        P("section", "tp"),
        P("tp"),
    )
    nz = mesh.shape["section"] // NY
    return jax.shard_map(
        functools.partial(shards, nz, 2), mesh=mesh, in_specs=placed,
        out_specs=(P("section", "tp"), P()), check_vma=False
    )
```

```python
import functools

import jax
import jax.numpy as jnp
from jax import lax
from jax.experimental import pallas as pl
from jax.experimental.pallas import tpu as pltpu
from jax.sharding import PartitionSpec as P

CAND = 32
NX, NY, NZ = 4, 4, 16
NW = 4
EPS = 1e-05
BF = jnp.bfloat16
F32 = jnp.float32
FAR = (0, 4, -4, 8)
NT = (((1,), (1,)), ((), ()))
MESH = pl.DeviceIdType.MESH


def split(v, parts):
    out = []
    for _ in range(parts):
        term = v.astype(BF)
        out.append(term)
        v = v - term.astype(F32)
    return out


def stacked(terms, rows):
    width = terms[0].shape[1]
    sub = lax.broadcasted_iota(jnp.int32, (rows, width), 0)
    out = jnp.zeros((rows, width), F32)
    for i, term in enumerate(terms):
        out = jnp.where(sub == i, term.astype(F32), out)
    return out.astype(BF)


def kernel(pa, prev_ref, owner_ref, gain_ref, wg_ref, wu_ref, wd_ref, sv_ref, out_ref, score_ref,
           x, wgu, wt, wd, vv, gus, guo, gub, rc, rx, hid, pt, r1p, r1q, r2p, r2q, fs, rf, ow, rsc, sc,
           lsem, ssem, rsem):
    rows, feats, hidden = prev_ref.shape[0], prev_ref.shape[1], wg_ref.shape[0]
    hpad = -(-hidden // 128) * 128
    full = hidden // 128 * 128
    rest = hidden - full
    width = 2 * hidden
    half, blk = 2 * NY * rows, 2 * NY * rows // NX
    A, B = pl.ds(0, pa), pl.ds(pa, feats - pa)
    s, t = lax.axis_index("section"), lax.axis_index("tp")
    yy, zz = s // NZ, s % NZ
    xx, cc = t // 2, t % 2
    near = (0, -1, 1, 2 * (1 - 2 * (zz % 2)))
    side = (0, -1, 1, 2)

    def dev(dx=0, dy=0, dz=0, other=False):
        core = 1 - cc if other else cc
        return (((yy + dy + NY) % NY) * NZ + (zz + dz + NZ) % NZ, ((xx + dx) % NX) * 2 + core)

    used = [0]
    flying = []

    def send(items, union):
        i = used[0]
        used[0] += 1
        for src, dst, to in items:
            pltpu.make_async_remote_copy(src_ref=src, dst_ref=dst, send_sem=ssem.at[i], recv_sem=rsem.at[i],
                                         device_id=to, device_id_type=MESH).start()
        whole = pltpu.make_async_remote_copy(src_ref=union, dst_ref=union, send_sem=ssem.at[i], recv_sem=rsem.at[i],
                                             device_id=items[0][2], device_id_type=MESH)
        flying.append(whole)
        return whole

    loads = []

    def load(src, dst):
        copy = pltpu.make_async_copy(src, dst, lsem.at[len(loads)])
        copy.start()
        loads.append(copy)

    if full:
        load(wg_ref.at[pl.ds(0, full)], wgu.at[pl.ds(0, full)])
        load(wu_ref.at[pl.ds(0, full)], wgu.at[pl.ds(full, full)])
    if rest:
        load(wg_ref.at[pl.ds(full, rest)], wgu.at[pl.ds(2 * full, rest)])
        load(wu_ref.at[pl.ds(full, rest)], wgu.at[pl.ds(2 * full + rest, rest)])
    load(wd_ref, wd.at[pl.ds(0, hidden)])
    if rest:
        wd[pl.ds(hidden, hpad - hidden), :] = jnp.zeros((hpad - hidden, feats), BF)
    x[0, 0, 0] = prev_ref[...]
    lane = lax.broadcasted_iota(jnp.int32, (1, 128), 1)
    mine = jnp.zeros((1, 128), jnp.int32)
    for r in range(rows):
        mine = jnp.where(lane % rows == r, owner_ref[r], mine)
    ow[0, 0, 0] = mine

    tp_peers = [dev(dx=dx, other=o) for dx in range(NX) for o in (False, True) if (dx, o) != (0, False)]
    y_peers = [dev(dy=dy) for dy in range(1, NY)]
    z_peers = [dev(dz=dz) for dz in range(1, NZ)]
    barrier = pltpu.get_barrier_semaphore()
    for peer in z_peers + y_peers + tp_peers:
        pl.semaphore_signal(barrier, inc=1, device_id=peer, device_id_type=MESH)
    pl.semaphore_wait(barrier, len(tp_peers + y_peers + z_peers))

    got = {}
    tasks = []

    def task(when):
        def add(fn):
            tasks.append((when, len(tasks), fn))
            return fn
        return add

    def spread(w):
        got["p2", w] = send([(x.at[w, 0, 0, :, A], x.at[w, 0, j, :, A], dev(dy=-side[j])) for j in (1, 2, 3)],
                            x.at[w, 0, pl.ds(1, 3), :, A])
        got["q2", w] = send([(x.at[w, 0, 0, :, B], x.at[w, n, 0, :, B], dev(dz=-near[n])) for n in (1, 2, 3)],
                            x.at[w, pl.ds(1, 3), 0, :, B])

    for w in (3, 1, 2):
        got["far", w] = send([(x.at[0, 0, 0], x.at[w, 0, 0], dev(dz=-FAR[w]))], x.at[w, 0, 0])
    spread(0)
    got["o1"] = send([(ow.at[0, 0, 0], ow.at[w, 0, 0], dev(dz=-FAR[w])) for w in (1, 2, 3)], ow.at[pl.ds(1, 3), 0, 0])

    begin = {0: 0.0, 1: 4.8, 2: 4.9, 3: 7.4}
    ready = {0: 8.0, 1: 12.0, 2: 14.0, 3: 16.5}

    for w in range(NW):
        if w:
            @task(begin[w])
            def _(w=w):
                got["far", w].wait_recv()
                spread(w)

        @task(begin[w] + 3.2)
        def _(w=w):
            got["p2", w].wait_recv()
            got["p3", w] = send([(x.at[w, 0, :, :, A], x.at[w, n, :, :, A], dev(dz=-near[n])) for n in (1, 2, 3)],
                                x.at[w, pl.ds(1, 3), :, :, A])

        @task(begin[w] + 3.3)
        def _(w=w):
            got["q2", w].wait_recv()
            got["q3", w] = send([(x.at[w, :, 0, :, B], x.at[w, :, j, :, B], dev(dy=-side[j])) for j in (1, 2, 3)],
                                x.at[w, :, pl.ds(1, 3), :, B])

    step = 128
    for i in range(width // step):
        @task(0.1 + 0.3 * i)
        def _(i=i):
            if i == 0:
                for copy in loads:
                    copy.wait()
            piece = wgu[pl.ds(i * step, step), :].astype(F32) * gain_ref[...]
            wt[:, pl.ds(i * step, step)] = piece.astype(BF).T

    svs = stacked(split(sv_ref[...], 3), 16)

    @task(5.5)
    def _():
        v = lax.dot_general(svs, wd[...], NT, preferred_element_type=F32)
        vv[...] = stacked(split(v[0:1] + v[1:2] + v[2:3], 3), 16)

    @task(9.0)
    def _():
        got["o1"].wait_recv()
        got["o2"] = send([(ow.at[:, 0, 0], ow.at[:, 0, j], dev(dy=-side[j])) for j in (1, 2, 3)],
                         ow.at[:, 0, pl.ds(1, 3)])

    @task(13.0)
    def _():
        got["o2"].wait_recv()
        got["o3"] = send([(ow.at[:, 0], ow.at[:, n], dev(dz=-near[n])) for n in (1, 2, 3)], ow.at[:, pl.ds(1, 3)])

    lane_h = lax.broadcasted_iota(jnp.int32, (half, 128), 1)

    def pair_tile(sq):
        hi, lo = split(sq, 2)
        return jnp.where(lane_h == 0, hi.astype(F32), jnp.where(lane_h == 1, lo.astype(F32), 0.0))

    def product(w, core):
        part = x[w, pl.ds(2 * core, 2)].reshape(half, feats)
        wide = part.astype(F32)
        sq = jnp.sum(wide * wide, axis=1, keepdims=True)
        return jnp.dot(part, wt[...], preferred_element_type=F32), pair_tile(sq)

    for w in range(NW):
        at = ready[w]

        @task(at)
        def _(w=w):
            got["p3", w].wait_recv()
            got["q3", w].wait_recv()
            gu, sq = product(w, 1 - cc)
            gus[w, :, pl.ds(0, width)] = gu.astype(BF)
            gus[w, :, pl.ds(width, 128)] = sq.astype(BF)
            got["c1", w] = send([(gus.at[w], rc.at[w], dev(other=True))], rc.at[w])
            gu, sq = product(w, cc)
            guo[w, :, :, pl.ds(0, width)] = gu.reshape(NX, blk, width)
            guo[w, :, :, pl.ds(width, 128)] = sq.reshape(NX, blk, 128)

        @task(at + 1.6)
        def _(w=w):
            got["c1", w].wait_recv()
            total = guo[w].reshape(half, width + 128) + rc[w].astype(F32)
            sq = pair_tile(total[:, width:width + 1] + total[:, width + 1:width + 2])
            guo[w, :, :, pl.ds(0, width)] = total[:, 0:width].reshape(NX, blk, width)
            guo[w, :, :, pl.ds(width, 128)] = sq.reshape(NX, blk, 128)
            gub[w, :, :, pl.ds(0, width)] = total[:, 0:width].astype(BF).reshape(NX, blk, width)
            gub[w, :, :, pl.ds(width, 128)] = sq.astype(BF).reshape(NX, blk, 128)
            got["x", w] = send([(gub.at[w, (xx + dx) % NX], rx.at[w, dx - 1], dev(dx=dx)) for dx in (2, 1, 3)], rx.at[w])

        @task(at + 5.6)
        def _(w=w):
            got["x", w].wait_recv()
            gu = guo[w, xx]
            for i in range(NX - 1):
                gu = gu + rx[w, i].astype(F32)
            sq = gu[:, width:width + 1] + gu[:, width + 1:width + 2]
            gu = gu[:, 0:width] * lax.rsqrt(sq / (feats * NX * 2) + EPS)

            def act(gate, up):
                return (gate / (1.0 + jnp.exp(-gate)) * up).astype(BF)

            if full:
                hid[w, cc, xx, :, pl.ds(0, full)] = act(gu[:, 0:full], gu[:, full:2 * full])
            if rest:
                last = gu[:, 2 * full:]
                at_lane = lax.broadcasted_iota(jnp.int32, last.shape, 1)
                value = act(last, pltpu.roll(last, 128 - rest, 1))
                hid[w, cc, xx, :, pl.ds(full, 128)] = jnp.where(at_lane < rest, value, jnp.zeros_like(value))
            done = hid.at[w, cc, xx]
            got["h", w] = send([(done, done, dev(dx=dx)) for dx in (2, 1, 3)], hid.at[w, cc, pl.ds(0, NX - 1)])

        @task(at + 9.4)
        def _(w=w):
            got["h", w].wait_recv()
            got["c2", w] = send([(hid.at[w, cc], hid.at[w, cc], dev(other=True))], hid.at[w, cc])

        @task(at + 10.4)
        def _(w=w):
            got["c2", w].wait_recv()
            act = hid[w].reshape(2 * half, hpad)
            down = jnp.dot(act, wd[...], preferred_element_type=F32)
            pt[w] = down.astype(BF).reshape(4, NY, rows, feats)
            got["r1p", w] = send([(pt.at[w, n, :, :, A], r1p.at[w, n - 1], dev(dz=near[n])) for n in (1, 2, 3)], r1p.at[w])
            got["r1q", w] = send([(pt.at[w, :, j, :, B], r1q.at[w, j - 1], dev(dy=side[j])) for j in (1, 2, 3)], r1q.at[w])
            v = lax.dot_general(vv[...], act, NT, preferred_element_type=F32)
            rsc[w] = v[0:8]

        @task(at + 15.0)
        def _(w=w):
            got["r1p", w].wait_recv()
            v = pt[w, 0, :, :, A].astype(F32)
            for i in range(3):
                v = v + r1p[w, i].astype(F32)
            pt[w, 0, :, :, A] = v.astype(BF)
            got["r2p", w] = send([(pt.at[w, 0, j, :, A], r2p.at[w, j - 1], dev(dy=side[j])) for j in (1, 2, 3)], r2p.at[w])

        @task(at + 15.1)
        def _(w=w):
            got["r1q", w].wait_recv()
            v = pt[w, :, 0, :, B].astype(F32)
            for i in range(3):
                v = v + r1q[w, i].astype(F32)
            pt[w, :, 0, :, B] = v.astype(BF)
            got["r2q", w] = send([(pt.at[w, n, 0, :, B], r2q.at[w, n - 1], dev(dz=near[n])) for n in (1, 2, 3)], r2q.at[w])

        @task(at + 18.8)
        def _(w=w):
            got["r2p", w].wait_recv()
            got["r2q", w].wait_recv()
            a, b = pt[w, 0, 0, :, A].astype(F32), pt[w, 0, 0, :, B].astype(F32)
            for i in range(3):
                a, b = a + r2p[w, i].astype(F32), b + r2q[w, i].astype(F32)
            fs[w, :, A] = a.astype(BF)
            fs[w, :, B] = b.astype(BF)
            if w:
                got["rf", w] = send([(fs.at[w], rf.at[w - 1], dev(dz=FAR[w]))], rf.at[w - 1])

    bases = (0, len(tp_peers) + 1, len(tp_peers) + len(y_peers) + 2)

    def exchange(key, base, value, peers):
        sc[base] = value
        got[key] = send([(sc.at[base], sc.at[base + 1 + i], peer) for i, peer in enumerate(peers)],
                        sc.at[pl.ds(base + 1, len(peers))])

    def collect(key, base, peers):
        got[key].wait_recv()
        v = sc[base]
        for i in range(len(peers)):
            v = v + sc[base + 1 + i]
        return v

    keep = {}
    last_d = ready[NW - 1] + 10.4

    @task(last_d + 0.1)
    def _():
        got["o3"].wait_recv()
        direct = lax.dot_general(svs, x[0, pl.ds(0, 2)].reshape(half, feats), NT, preferred_element_type=F32)
        direct = jnp.where(lane < rows, direct[0:1] + direct[1:2] + direct[2:3], 0.0)
        cand = lax.broadcasted_iota(jnp.int32, (128, 128), 0)
        per = 128 // rows
        sums = jnp.zeros((16, 128), F32)
        for w in range(NW):
            for h in range(2):
                who = jnp.zeros((1, 128), jnp.int32)
                for p in range(per):
                    who = jnp.where(lane // rows == p, ow[w, 2 * h + p // NY, p % NY], who)
                score = rsc[w, :, pl.ds(h * 128, 128)]
                score = score[0:1] + score[1:2] + score[2:3]
                if w == 0 and h == 0:
                    score = score + direct
                terms = stacked(split(score, 3) + [jnp.ones((1, 128), BF)], 16)
                sums = sums + lax.dot_general(terms, jnp.where(cand == who, 1.0, 0.0).astype(BF), NT,
                                              preferred_element_type=F32)
        keep["count"] = sums[3:4]
        exchange("s1", bases[0], sums[0:1] + sums[1:2] + sums[2:3], tp_peers)

    @task(last_d + 4.5)
    def _():
        exchange("s2", bases[1], collect("s1", bases[0], tp_peers), y_peers)

    @task(last_d + 8.3)
    def _():
        exchange("s3", bases[2], collect("s2", bases[1], y_peers), z_peers)

    for _, _, fn in sorted(tasks, key=lambda item: item[:2]):
        fn()

    v = fs[0].astype(F32)
    for w in range(1, NW):
        got["rf", w].wait_recv()
        v = v + rf[w - 1].astype(F32)
    out_ref[...] = (v + prev_ref[...].astype(F32)).astype(BF)
    assert used[0] == ssem.shape[0]
    score_ref[...] = collect("s3", bases[2], z_peers) / keep["count"]
    for copy in flying:
        copy.wait_send()


def shards(preview, row_owner, norm_gain, w_gate, w_up, w_down, score_vec):
    rows, feats = preview.shape
    hidden = w_gate.shape[0]
    hpad = -(-hidden // 128) * 128
    half, blk, wide = 2 * NY * rows, 2 * NY * rows // NX, 2 * hidden + 128
    pa = max(1, feats // 128 * 3 // 8) * 128
    pb = feats - pa
    sems = 60
    vmem = pl.BlockSpec(memory_space=pltpu.VMEM)
    hbm = pl.BlockSpec(memory_space=pl.ANY)
    verified, scores = pl.pallas_call(
        functools.partial(kernel, pa),
        out_shape=(jax.ShapeDtypeStruct((rows, feats), BF), jax.ShapeDtypeStruct((1, 128), F32)),
        in_specs=[vmem, pl.BlockSpec(memory_space=pltpu.SMEM), vmem, hbm, hbm, hbm, vmem],
        out_specs=(vmem, vmem),
        scratch_shapes=[
            pltpu.VMEM((NW, 4, NY, rows, feats), BF),
            pltpu.VMEM((2 * hidden, feats), BF),
            pltpu.VMEM((feats, 2 * hidden), BF),
            pltpu.VMEM((hpad, feats), BF),
            pltpu.VMEM((16, hpad), BF),
            pltpu.VMEM((NW, half, wide), BF),
            pltpu.VMEM((NW, NX, blk, wide), F32),
            pltpu.VMEM((NW, NX, blk, wide), BF),
            pltpu.VMEM((NW, half, wide), BF),
            pltpu.VMEM((NW, NX - 1, blk, wide), BF),
            pltpu.VMEM((NW, 2, NX, blk, hpad), BF),
            pltpu.VMEM((NW, 4, NY, rows, feats), BF),
            pltpu.VMEM((NW, 3, NY, rows, pa), BF),
            pltpu.VMEM((NW, 3, 4, rows, pb), BF),
            pltpu.VMEM((NW, 3, rows, pa), BF),
            pltpu.VMEM((NW, 3, rows, pb), BF),
            pltpu.VMEM((NW, rows, feats), BF),
            pltpu.VMEM((NW - 1, rows, feats), BF),
            pltpu.VMEM((NW, 4, NY, 1, 128), jnp.int32),
            pltpu.VMEM((NW, 8, 2 * half), F32),
            pltpu.VMEM((2 * NX + NY + NZ, 1, 128), F32),
            pltpu.SemaphoreType.DMA((5,)),
            pltpu.SemaphoreType.DMA((sems,)),
            pltpu.SemaphoreType.DMA((sems,)),
        ],
        compiler_params=pltpu.CompilerParams(
            collective_id=0, has_side_effects=True, vmem_limit_bytes=56 << 20),
    )(preview, row_owner, norm_gain[None, :], w_gate, w_up, w_down, score_vec[None, :])
    return verified, scores[0, :CAND]


def solution(mesh):
    placed = (
        P("section", "tp"),
        P("section"),
        P("tp"),
        P("section", "tp"),
        P("section", "tp"),
        P("section", "tp"),
        P("tp"),
    )
    return jax.shard_map(
        shards, mesh=mesh, in_specs=placed, out_specs=(P("section", "tp"), P()), check_vma=False
    )
```

```python
import functools

import jax
import jax.numpy as jnp
from jax import lax
from jax.experimental import pallas as pl
from jax.experimental.pallas import tpu as pltpu
from jax.sharding import PartitionSpec as P

CAND = 32
NX, NY, NZ = 4, 4, 16
NW = 4
EPS = 1e-05
BF = jnp.bfloat16
F32 = jnp.float32
FAR = (0, 4, -4, 8)
NT = (((1,), (1,)), ((), ()))
MESH = pl.DeviceIdType.MESH
ORDER = (
    "far2", "far3", "nq", "wts", "s0", "far1", "nrm", "s2", "p0", "q0", "s1", "s3",
    "q2", "p2", "vec", "m0", "own2", "q3", "p3", "x0", "own3", "p1", "m2", "q1",
    "x2", "m3", "h0", "x3", "m1", "h2", "x1", "h3", "c0", "c2", "d0", "d2",
    "h1", "c3", "d3", "c1", "d1", "v1", "f3", "e3", "e0", "f0", "f2", "e2",
    "v2", "f1", "e1", "g3", "g0", "v3", "g1", "g2",
)


def split(v, parts):
    out = []
    for _ in range(parts):
        term = v.astype(BF)
        out.append(term)
        v = v - term.astype(F32)
    return out


def stacked(terms, rows):
    width = terms[0].shape[1]
    sub = lax.broadcasted_iota(jnp.int32, (rows, width), 0)
    out = jnp.zeros((rows, width), F32)
    for i, term in enumerate(terms):
        out = jnp.where(sub == i, term.astype(F32), out)
    return out.astype(BF)


def kernel(pa, prev_hbm, owner_ref, gain_hbm, wg_ref, wu_ref, wd_ref, sv_hbm, out_ref, score_ref,
           prev_ref, gain_ref, sv_ref, x, wgu, wt, wd, vv, sv3, nq, gus, guo, gub, rc, rx, hid, pt, r1p, r1q, r2p, r2q, fs, rf, ow, rsc, sc,
           lsem, ssem, rsem):
    rows, feats, hidden = prev_hbm.shape[0], prev_hbm.shape[1], wg_ref.shape[0]
    hpad = -(-hidden // 128) * 128
    full = hidden // 128 * 128
    rest = hidden - full
    width = 2 * hidden
    half, blk = 2 * NY * rows, 2 * NY * rows // NX
    A, B = pl.ds(0, pa), pl.ds(pa, feats - pa)
    s, t = lax.axis_index("section"), lax.axis_index("tp")
    yy, zz = s // NZ, s % NZ
    xx, cc = t // 2, t % 2
    near = (0, -1, 1, 2 * (1 - 2 * (zz % 2)))
    side = (0, -1, 1, 2)

    def dev(dx=0, dy=0, dz=0, other=False):
        core = 1 - cc if other else cc
        return (((yy + dy + NY) % NY) * NZ + (zz + dz + NZ) % NZ, ((xx + dx) % NX) * 2 + core)

    used = [0]
    flying = []

    def send(items, union):
        i = used[0]
        used[0] += 1
        for src, dst, to in items:
            pltpu.make_async_remote_copy(src_ref=src, dst_ref=dst, send_sem=ssem.at[i], recv_sem=rsem.at[i],
                                         device_id=to, device_id_type=MESH).start()
        whole = pltpu.make_async_remote_copy(src_ref=union, dst_ref=union, send_sem=ssem.at[i], recv_sem=rsem.at[i],
                                             device_id=items[0][2], device_id_type=MESH)
        flying.append(whole)
        return whole

    tp_peers = [dev(dx=dx, other=o) for dx in range(NX) for o in (False, True) if (dx, o) != (0, False)]
    y_peers = [dev(dy=dy) for dy in range(1, NY)]
    z_peers = [dev(dz=dz) for dz in range(1, NZ)]
    barrier = pltpu.get_barrier_semaphore()
    for peer in z_peers + y_peers + tp_peers:
        pl.semaphore_signal(barrier, inc=1, device_id=peer, device_id_type=MESH)
    loads = []

    def load(src, dst):
        copy = pltpu.make_async_copy(src, dst, lsem.at[len(loads)])
        copy.start()
        loads.append(copy)

    load(prev_hbm, prev_ref)
    load(gain_hbm, gain_ref)
    load(sv_hbm, sv_ref)
    if full:
        load(wg_ref.at[pl.ds(0, full)], wgu.at[pl.ds(0, full)])
        load(wu_ref.at[pl.ds(0, full)], wgu.at[pl.ds(full, full)])
    if rest:
        load(wg_ref.at[pl.ds(full, rest)], wgu.at[pl.ds(2 * full, rest)])
        load(wu_ref.at[pl.ds(full, rest)], wgu.at[pl.ds(2 * full + rest, rest)])
    load(wd_ref, wd.at[pl.ds(0, hidden)])
    if rest:
        wd[pl.ds(hidden, hpad - hidden), :] = jnp.zeros((hpad - hidden, feats), BF)
    loads[0].wait()
    x[0, 0, 0] = prev_ref[...]
    lane = lax.broadcasted_iota(jnp.int32, (1, 128), 1)
    owner = jnp.zeros((1, 128), F32)
    for r in range(rows):
        owner = jnp.where(lane % rows == r, owner_ref[r].astype(F32), owner)
    own = prev_ref[...].astype(F32)
    sq = jnp.sum(own * own, axis=1, keepdims=True)
    eye = (lax.broadcasted_iota(jnp.int32, (rows, 128), 1) % rows
           == lax.broadcasted_iota(jnp.int32, (rows, 128), 0))
    nq[0] = jnp.sum(jnp.where(eye, sq, 0.0), axis=0, keepdims=True)
    pl.semaphore_wait(barrier, len(tp_peers + y_peers + z_peers))

    got = {}
    tasks = {}

    def task(name):
        def add(fn):
            tasks[name] = fn
            return fn
        return add

    def spread(w):
        got["p2", w] = send([(x.at[w, 0, 0, :, A], x.at[w, 0, j, :, A], dev(dy=-side[j])) for j in (1, 2, 3)],
                            x.at[w, 0, pl.ds(1, 3), :, A])
        got["q2", w] = send([(x.at[w, 0, 0, :, B], x.at[w, n, 0, :, B], dev(dz=-near[n])) for n in (1, 2, 3)],
                            x.at[w, pl.ds(1, 3), 0, :, B])

    for w in range(NW):
        if w:
            @task(f"far{w}")
            def _(w=w):
                got["far", w] = send([(x.at[0, 0, 0], x.at[w, 0, 0], dev(dz=-FAR[w]))], x.at[w, 0, 0])

        @task(f"s{w}")
        def _(w=w):
            if w:
                got["far", w].wait_recv()
            spread(w)

        @task(f"p{w}")
        def _(w=w):
            got["p2", w].wait_recv()
            got["p3", w] = send([(x.at[w, 0, :, :, A], x.at[w, n, :, :, A], dev(dz=-near[n])) for n in (1, 2, 3)],
                                x.at[w, pl.ds(1, 3), :, :, A])

        @task(f"q{w}")
        def _(w=w):
            got["q2", w].wait_recv()
            got["q3", w] = send([(x.at[w, :, 0, :, B], x.at[w, :, j, :, B], dev(dy=-side[j])) for j in (1, 2, 3)],
                                x.at[w, :, pl.ds(1, 3), :, B])

    @task("nq")
    def _():
        got["nq"] = send([(nq.at[0], nq.at[i + 1], peer) for i, peer in enumerate(tp_peers)],
                         nq.at[pl.ds(1, len(tp_peers))])

    @task("nrm")
    def _():
        got["nq"].wait_recv()
        total = nq[0]
        for i in range(len(tp_peers)):
            total = total + nq[i + 1]
        ow[0, 0, 0, 0:1] = owner
        ow[0, 0, 0, 1:2] = lax.rsqrt(total / (feats * NX * 2) + EPS)
        got["o1"] = send([(ow.at[0, 0, 0], ow.at[w, 0, 0], dev(dz=-FAR[w])) for w in (1, 2, 3)],
                         ow.at[pl.ds(1, 3), 0, 0])

    @task("own2")
    def _():
        got["o1"].wait_recv()
        got["o2"] = send([(ow.at[:, 0, 0], ow.at[:, 0, j], dev(dy=-side[j])) for j in (1, 2, 3)],
                         ow.at[:, 0, pl.ds(1, 3)])

    @task("own3")
    def _():
        got["o2"].wait_recv()
        got["o3"] = send([(ow.at[:, 0], ow.at[:, n], dev(dz=-near[n])) for n in (1, 2, 3)], ow.at[:, pl.ds(1, 3)])

    have = []

    def owners():
        if not have:
            got["o3"].wait_recv()
            have.append(True)

    step = 128

    @task("wts")
    def _():
        for copy in loads[1:]:
            copy.wait()
        for i in range(width // step):
            piece = wgu[pl.ds(i * step, step), :].astype(F32) * gain_ref[...]
            wt[:, pl.ds(i * step, step)] = piece.astype(BF).T

    @task("vec")
    def _():
        sv3[...] = stacked(split(sv_ref[...], 3), 16)
        v = lax.dot_general(sv3[...], wd[...], NT, preferred_element_type=F32)
        vv[...] = stacked(split(v[0:1] + v[1:2] + v[2:3], 3), 16)

    def product(w, core):
        part = x[w, pl.ds(2 * core, 2)].reshape(half, feats)
        return jnp.dot(part, wt[...], preferred_element_type=F32)

    for w in range(NW):
        @task(f"m{w}")
        def _(w=w):
            got["p3", w].wait_recv()
            got["q3", w].wait_recv()
            gus[w] = product(w, 1 - cc).astype(BF)
            got["c1", w] = send([(gus.at[w], rc.at[w], dev(other=True))], rc.at[w])
            guo[w] = product(w, cc).reshape(NX, blk, width)

        @task(f"x{w}")
        def _(w=w):
            got["c1", w].wait_recv()
            total = guo[w] + rc[w].astype(F32).reshape(NX, blk, width)
            guo[w] = total
            gub[w] = total.astype(BF)
            got["x", w] = send([(gub.at[w, (xx + dx) % NX], rx.at[w, dx - 1], dev(dx=dx)) for dx in (2, 1, 3)], rx.at[w])

        @task(f"h{w}")
        def _(w=w):
            owners()
            got["x", w].wait_recv()
            gu = guo[w, xx]
            for i in range(NX - 1):
                gu = gu + rx[w, i].astype(F32)
            scales = [ow[w, 2 * cc + xx // 2, 2 * (xx % 2) + i][1:2] for i in range(2)]
            scale = jnp.concatenate([jnp.sum(jnp.where(eye & (lane < rows), sc_, 0.0), axis=1, keepdims=True)
                                     for sc_ in scales], axis=0)
            gu = gu * scale

            def act(gate, up):
                return (gate / (1.0 + jnp.exp(-gate)) * up).astype(BF)

            if full:
                hid[w, cc, xx, :, pl.ds(0, full)] = act(gu[:, 0:full], gu[:, full:2 * full])
            if rest:
                last = gu[:, 2 * full:]
                at_lane = lax.broadcasted_iota(jnp.int32, last.shape, 1)
                value = act(last, pltpu.roll(last, 128 - rest, 1))
                hid[w, cc, xx, :, pl.ds(full, 128)] = jnp.where(at_lane < rest, value, jnp.zeros_like(value))
            done = hid.at[w, cc, xx]
            got["h", w] = send([(done, done, dev(dx=dx)) for dx in (2, 1, 3)], hid.at[w, cc, pl.ds(0, NX - 1)])

        @task(f"c{w}")
        def _(w=w):
            got["h", w].wait_recv()
            got["c2", w] = send([(hid.at[w, cc], hid.at[w, cc], dev(other=True))], hid.at[w, cc])

        @task(f"d{w}")
        def _(w=w):
            got["c2", w].wait_recv()
            act = hid[w].reshape(2 * half, hpad)
            down = jnp.dot(act, wd[...], preferred_element_type=F32)
            pt[w] = down.astype(BF).reshape(4, NY, rows, feats)
            got["r1p", w] = send([(pt.at[w, n, :, :, A], r1p.at[w, n - 1], dev(dz=near[n])) for n in (1, 2, 3)], r1p.at[w])
            got["r1q", w] = send([(pt.at[w, :, j, :, B], r1q.at[w, j - 1], dev(dy=side[j])) for j in (1, 2, 3)], r1q.at[w])
            v = lax.dot_general(vv[...], act, NT, preferred_element_type=F32)
            rsc[w] = v[0:8]

        @task(f"e{w}")
        def _(w=w):
            got["r1p", w].wait_recv()
            v = pt[w, 0, :, :, A].astype(F32)
            for i in range(3):
                v = v + r1p[w, i].astype(F32)
            pt[w, 0, :, :, A] = v.astype(BF)
            got["r2p", w] = send([(pt.at[w, 0, j, :, A], r2p.at[w, j - 1], dev(dy=side[j])) for j in (1, 2, 3)], r2p.at[w])

        @task(f"f{w}")
        def _(w=w):
            got["r1q", w].wait_recv()
            v = pt[w, :, 0, :, B].astype(F32)
            for i in range(3):
                v = v + r1q[w, i].astype(F32)
            pt[w, :, 0, :, B] = v.astype(BF)
            got["r2q", w] = send([(pt.at[w, n, 0, :, B], r2q.at[w, n - 1], dev(dz=near[n])) for n in (1, 2, 3)], r2q.at[w])

        @task(f"g{w}")
        def _(w=w):
            got["r2p", w].wait_recv()
            got["r2q", w].wait_recv()
            a, b = pt[w, 0, 0, :, A].astype(F32), pt[w, 0, 0, :, B].astype(F32)
            for i in range(3):
                a, b = a + r2p[w, i].astype(F32), b + r2q[w, i].astype(F32)
            fs[w, :, A] = a.astype(BF)
            fs[w, :, B] = b.astype(BF)
            if w:
                got["rf", w] = send([(fs.at[w], rf.at[w - 1], dev(dz=FAR[w]))], rf.at[w - 1])

    bases = (0, len(tp_peers) + 1, len(tp_peers) + len(y_peers) + 2)

    def exchange(key, base, value, peers):
        sc[base] = value
        got[key] = send([(sc.at[base], sc.at[base + 1 + i], peer) for i, peer in enumerate(peers)],
                        sc.at[pl.ds(base + 1, len(peers))])

    def collect(key, base, peers):
        got[key].wait_recv()
        v = sc[base]
        for i in range(len(peers)):
            v = v + sc[base + 1 + i]
        return v

    keep = {}
    @task("v1")
    def _():
        owners()
        direct = lax.dot_general(sv3[...], x[0, pl.ds(0, 2)].reshape(half, feats), NT, preferred_element_type=F32)
        direct = jnp.where(lane < rows, direct[0:1] + direct[1:2] + direct[2:3], 0.0)
        cand = lax.broadcasted_iota(jnp.int32, (128, 128), 0).astype(F32)
        per = 128 // rows
        sums = jnp.zeros((16, 128), F32)
        for w in range(NW):
            for h in range(2):
                who = jnp.zeros((1, 128), F32)
                for p in range(per):
                    who = jnp.where(lane // rows == p, ow[w, 2 * h + p // NY, p % NY][0:1], who)
                score = rsc[w, :, pl.ds(h * 128, 128)]
                score = score[0:1] + score[1:2] + score[2:3]
                if w == 0 and h == 0:
                    score = score + direct
                terms = stacked(split(score, 3) + [jnp.ones((1, 128), BF)], 16)
                sums = sums + lax.dot_general(terms, jnp.where(cand == who, 1.0, 0.0).astype(BF), NT,
                                              preferred_element_type=F32)
        keep["count"] = sums[3:4]
        exchange("s1", bases[0], sums[0:1] + sums[1:2] + sums[2:3], tp_peers)

    @task("v2")
    def _():
        exchange("s2", bases[1], collect("s1", bases[0], tp_peers), y_peers)

    @task("v3")
    def _():
        exchange("s3", bases[2], collect("s2", bases[1], y_peers), z_peers)

    assert sorted(ORDER) == sorted(tasks)
    for name in ORDER:
        tasks[name]()

    v = fs[0].astype(F32)
    for w in range(1, NW):
        got["rf", w].wait_recv()
        v = v + rf[w - 1].astype(F32)
    out_ref[...] = (v + prev_ref[...].astype(F32)).astype(BF)
    assert used[0] == ssem.shape[0]
    score_ref[...] = collect("s3", bases[2], z_peers) / keep["count"]
    for copy in flying:
        copy.wait_send()


def shards(preview, row_owner, norm_gain, w_gate, w_up, w_down, score_vec):
    rows, feats = preview.shape
    hidden = w_gate.shape[0]
    hpad = -(-hidden // 128) * 128
    half, blk, wide = 2 * NY * rows, 2 * NY * rows // NX, 2 * hidden
    pa = feats // 256 * 128
    pb = feats - pa
    sems = 61
    vmem = pl.BlockSpec(memory_space=pltpu.VMEM)
    hbm = pl.BlockSpec(memory_space=pl.ANY)
    verified, scores = pl.pallas_call(
        functools.partial(kernel, pa),
        out_shape=(jax.ShapeDtypeStruct((rows, feats), BF), jax.ShapeDtypeStruct((1, 128), F32)),
        in_specs=[hbm, pl.BlockSpec(memory_space=pltpu.SMEM), hbm, hbm, hbm, hbm, hbm],
        out_specs=(vmem, vmem),
        scratch_shapes=[
            pltpu.VMEM((rows, feats), BF),
            pltpu.VMEM((1, feats), F32),
            pltpu.VMEM((1, feats), F32),
            pltpu.VMEM((NW, 4, NY, rows, feats), BF),
            pltpu.VMEM((2 * hidden, feats), BF),
            pltpu.VMEM((feats, 2 * hidden), BF),
            pltpu.VMEM((hpad, feats), BF),
            pltpu.VMEM((16, hpad), BF),
            pltpu.VMEM((16, feats), BF),
            pltpu.VMEM((2 * NX, 1, 128), F32),
            pltpu.VMEM((NW, half, wide), BF),
            pltpu.VMEM((NW, NX, blk, wide), F32),
            pltpu.VMEM((NW, NX, blk, wide), BF),
            pltpu.VMEM((NW, half, wide), BF),
            pltpu.VMEM((NW, NX - 1, blk, wide), BF),
            pltpu.VMEM((NW, 2, NX, blk, hpad), BF),
            pltpu.VMEM((NW, 4, NY, rows, feats), BF),
            pltpu.VMEM((NW, 3, NY, rows, pa), BF),
            pltpu.VMEM((NW, 3, 4, rows, pb), BF),
            pltpu.VMEM((NW, 3, rows, pa), BF),
            pltpu.VMEM((NW, 3, rows, pb), BF),
            pltpu.VMEM((NW, rows, feats), BF),
            pltpu.VMEM((NW - 1, rows, feats), BF),
            pltpu.VMEM((NW, 4, NY, 2, 128), F32),
            pltpu.VMEM((NW, 8, 2 * half), F32),
            pltpu.VMEM((2 * NX + NY + NZ, 1, 128), F32),
            pltpu.SemaphoreType.DMA((8,)),
            pltpu.SemaphoreType.DMA((sems,)),
            pltpu.SemaphoreType.DMA((sems,)),
        ],
        compiler_params=pltpu.CompilerParams(
            collective_id=0, has_side_effects=True, vmem_limit_bytes=56 << 20),
    )(preview, row_owner, norm_gain[None, :], w_gate, w_up, w_down, score_vec[None, :])
    return verified, scores[0, :CAND]


def solution(mesh):
    placed = (
        P("section", "tp"),
        P("section"),
        P("tp"),
        P("section", "tp"),
        P("section", "tp"),
        P("section", "tp"),
        P("tp"),
    )
    return jax.shard_map(
        shards, mesh=mesh, in_specs=placed, out_specs=(P("section", "tp"), P()), check_vma=False
    )
```

```python
import functools

import jax
import jax.numpy as jnp
from jax import lax
from jax.experimental import pallas as pl
from jax.experimental.pallas import tpu as pltpu
from jax.sharding import PartitionSpec as P

CAND = 32
NX, NY, NZ = 4, 4, 16
NW = 4
EPS = 1e-05
BF = jnp.bfloat16
F32 = jnp.float32
FAR = (0, 4, -4, 8)
NT = (((1,), (1,)), ((), ()))
MESH = pl.DeviceIdType.MESH
ORDER = (
    "far2", "nq", "wts", "far3", "s0", "far1", "nrm", "s2", "p0", "q0", "s1", "s3",
    "q2", "vec", "p2", "own2", "m0", "q3", "q1", "p3", "x0", "m2", "own3", "p1",
    "x2", "m3", "h0", "x3", "m1", "h2", "c0", "x1", "h3", "d0", "c2", "d2",
    "h1", "c3", "d3", "c1", "f2", "d1", "v1", "f3", "e3", "f0", "e2", "v2",
    "f1", "g3", "e1", "e0", "v3", "g2", "g1", "g0",
)


def split(v, parts):
    out = []
    for _ in range(parts):
        term = v.astype(BF)
        out.append(term)
        v = v - term.astype(F32)
    return out


def stacked(terms, rows):
    width = terms[0].shape[1]
    sub = lax.broadcasted_iota(jnp.int32, (rows, width), 0)
    out = jnp.zeros((rows, width), F32)
    for i, term in enumerate(terms):
        out = jnp.where(sub == i, term.astype(F32), out)
    return out.astype(BF)


def kernel(pa, prev_hbm, owner_ref, gain_hbm, wg_ref, wu_ref, wd_ref, sv_hbm, out_ref, score_ref,
           prev_ref, gain_ref, sv_ref, x, wgu, wt, wd, vv, sv3, nq, gus, guo, gub, rc, rx, hid, pt, r1p, r1q, r2p, r2q, fs, rf, ow, rsc, sc,
           lsem, ssem, rsem):
    rows, feats, hidden = prev_hbm.shape[0], prev_hbm.shape[1], wg_ref.shape[0]
    hpad = -(-hidden // 128) * 128
    full = hidden // 128 * 128
    rest = hidden - full
    width = 2 * hidden
    half, blk = 2 * NY * rows, 2 * NY * rows // NX
    A, B = pl.ds(0, pa), pl.ds(pa, feats - pa)
    s, t = lax.axis_index("section"), lax.axis_index("tp")
    yy, zz = s // NZ, s % NZ
    xx, cc = t // 2, t % 2
    near = (0, -1, 1, 2 * (1 - 2 * (zz % 2)))
    side = (0, -1, 1, 2)

    def dev(dx=0, dy=0, dz=0, other=False):
        core = 1 - cc if other else cc
        return (((yy + dy + NY) % NY) * NZ + (zz + dz + NZ) % NZ, ((xx + dx) % NX) * 2 + core)

    used = [0]
    flying = []

    def send(items, union):
        i = used[0]
        used[0] += 1
        for src, dst, to in items:
            pltpu.make_async_remote_copy(src_ref=src, dst_ref=dst, send_sem=ssem.at[i], recv_sem=rsem.at[i],
                                         device_id=to, device_id_type=MESH).start()
        whole = pltpu.make_async_remote_copy(src_ref=union, dst_ref=union, send_sem=ssem.at[i], recv_sem=rsem.at[i],
                                             device_id=items[0][2], device_id_type=MESH)
        flying.append(whole)
        return whole

    tp_peers = [dev(dx=dx, other=o) for dx in range(NX) for o in (False, True) if (dx, o) != (0, False)]
    y_peers = [dev(dy=dy) for dy in range(1, NY)]
    z_peers = [dev(dz=dz) for dz in range(1, NZ)]
    barrier = pltpu.get_barrier_semaphore()
    for peer in z_peers + y_peers + tp_peers:
        pl.semaphore_signal(barrier, inc=1, device_id=peer, device_id_type=MESH)
    loads = []

    def load(src, dst):
        copy = pltpu.make_async_copy(src, dst, lsem.at[len(loads)])
        copy.start()
        loads.append(copy)

    load(prev_hbm, prev_ref)
    load(gain_hbm, gain_ref)
    load(sv_hbm, sv_ref)
    if full:
        load(wg_ref.at[pl.ds(0, full)], wgu.at[pl.ds(0, full)])
        load(wu_ref.at[pl.ds(0, full)], wgu.at[pl.ds(full, full)])
    if rest:
        load(wg_ref.at[pl.ds(full, rest)], wgu.at[pl.ds(2 * full, rest)])
        load(wu_ref.at[pl.ds(full, rest)], wgu.at[pl.ds(2 * full + rest, rest)])
    load(wd_ref, wd.at[pl.ds(0, hidden)])
    if rest:
        wd[pl.ds(hidden, hpad - hidden), :] = jnp.zeros((hpad - hidden, feats), BF)
    loads[0].wait()
    x[0, 0, 0] = prev_ref[...]
    lane = lax.broadcasted_iota(jnp.int32, (1, 128), 1)
    owner = jnp.zeros((1, 128), F32)
    for r in range(rows):
        owner = jnp.where(lane % rows == r, owner_ref[r].astype(F32), owner)
    own = prev_ref[...].astype(F32)
    sq = jnp.sum(own * own, axis=1, keepdims=True)
    eye = (lax.broadcasted_iota(jnp.int32, (rows, 128), 1) % rows
           == lax.broadcasted_iota(jnp.int32, (rows, 128), 0))
    nq[0] = jnp.sum(jnp.where(eye, sq, 0.0), axis=0, keepdims=True)
    pl.semaphore_wait(barrier, len(tp_peers + y_peers + z_peers))

    got = {}
    tasks = {}

    def task(name):
        def add(fn):
            tasks[name] = fn
            return fn
        return add

    def spread(w):
        got["p2", w] = send([(x.at[w, 0, 0, :, A], x.at[w, 0, j, :, A], dev(dy=-side[j])) for j in (1, 2, 3)],
                            x.at[w, 0, pl.ds(1, 3), :, A])
        got["q2", w] = send([(x.at[w, 0, 0, :, B], x.at[w, n, 0, :, B], dev(dz=-near[n])) for n in (1, 2, 3)],
                            x.at[w, pl.ds(1, 3), 0, :, B])

    for w in range(NW):
        if w:
            @task(f"far{w}")
            def _(w=w):
                got["far", w] = send([(x.at[0, 0, 0], x.at[w, 0, 0], dev(dz=-FAR[w]))], x.at[w, 0, 0])

        @task(f"s{w}")
        def _(w=w):
            if w:
                got["far", w].wait_recv()
            spread(w)

        @task(f"p{w}")
        def _(w=w):
            got["p2", w].wait_recv()
            got["p3", w] = send([(x.at[w, 0, :, :, A], x.at[w, n, :, :, A], dev(dz=-near[n])) for n in (1, 2, 3)],
                                x.at[w, pl.ds(1, 3), :, :, A])

        @task(f"q{w}")
        def _(w=w):
            got["q2", w].wait_recv()
            got["q3", w] = send([(x.at[w, :, 0, :, B], x.at[w, :, j, :, B], dev(dy=-side[j])) for j in (1, 2, 3)],
                                x.at[w, :, pl.ds(1, 3), :, B])

    @task("nq")
    def _():
        got["nq"] = send([(nq.at[0], nq.at[i + 1], peer) for i, peer in enumerate(tp_peers)],
                         nq.at[pl.ds(1, len(tp_peers))])

    @task("nrm")
    def _():
        got["nq"].wait_recv()
        total = nq[0]
        for i in range(len(tp_peers)):
            total = total + nq[i + 1]
        ow[0, 0, 0, 0:1] = owner
        ow[0, 0, 0, 1:2] = lax.rsqrt(total / (feats * NX * 2) + EPS)
        got["o1"] = send([(ow.at[0, 0, 0], ow.at[w, 0, 0], dev(dz=-FAR[w])) for w in (1, 2, 3)],
                         ow.at[pl.ds(1, 3), 0, 0])

    @task("own2")
    def _():
        got["o1"].wait_recv()
        got["o2"] = send([(ow.at[:, 0, 0], ow.at[:, 0, j], dev(dy=-side[j])) for j in (1, 2, 3)],
                         ow.at[:, 0, pl.ds(1, 3)])

    @task("own3")
    def _():
        got["o2"].wait_recv()
        got["o3"] = send([(ow.at[:, 0], ow.at[:, n], dev(dz=-near[n])) for n in (1, 2, 3)], ow.at[:, pl.ds(1, 3)])

    have = []

    def owners():
        if not have:
            got["o3"].wait_recv()
            have.append(True)

    step = 128

    @task("wts")
    def _():
        for copy in loads[1:]:
            copy.wait()
        for i in range(width // step):
            piece = wgu[pl.ds(i * step, step), :].astype(F32) * gain_ref[...]
            wt[:, pl.ds(i * step, step)] = piece.astype(BF).T

    @task("vec")
    def _():
        sv3[...] = stacked(split(sv_ref[...], 3), 16)
        v = lax.dot_general(sv3[...], wd[...], NT, preferred_element_type=F32)
        vv[...] = stacked(split(v[0:1] + v[1:2] + v[2:3], 3), 16)

    def product(w, core):
        part = x[w, pl.ds(2 * core, 2)].reshape(half, feats)
        return jnp.dot(part, wt[...], preferred_element_type=F32)

    for w in range(NW):
        @task(f"m{w}")
        def _(w=w):
            got["p3", w].wait_recv()
            got["q3", w].wait_recv()
            gus[w] = product(w, 1 - cc).astype(BF)
            got["c1", w] = send([(gus.at[w], rc.at[w], dev(other=True))], rc.at[w])
            guo[w] = product(w, cc).reshape(NX, blk, width)

        @task(f"x{w}")
        def _(w=w):
            got["c1", w].wait_recv()
            total = guo[w] + rc[w].astype(F32).reshape(NX, blk, width)
            guo[w] = total
            gub[w] = total.astype(BF)
            got["x", w] = send([(gub.at[w, (xx + dx) % NX], rx.at[w, dx - 1], dev(dx=dx)) for dx in (2, 1, 3)], rx.at[w])

        @task(f"h{w}")
        def _(w=w):
            owners()
            got["x", w].wait_recv()
            gu = guo[w, xx]
            for i in range(NX - 1):
                gu = gu + rx[w, i].astype(F32)
            scales = [ow[w, 2 * cc + xx // 2, 2 * (xx % 2) + i][1:2] for i in range(2)]
            scale = jnp.concatenate([jnp.sum(jnp.where(eye & (lane < rows), sc_, 0.0), axis=1, keepdims=True)
                                     for sc_ in scales], axis=0)
            gu = gu * scale

            def act(gate, up):
                return (gate / (1.0 + jnp.exp(-gate)) * up).astype(BF)

            if full:
                hid[w, cc, xx, :, pl.ds(0, full)] = act(gu[:, 0:full], gu[:, full:2 * full])
            if rest:
                last = gu[:, 2 * full:]
                at_lane = lax.broadcasted_iota(jnp.int32, last.shape, 1)
                value = act(last, pltpu.roll(last, 128 - rest, 1))
                hid[w, cc, xx, :, pl.ds(full, 128)] = jnp.where(at_lane < rest, value, jnp.zeros_like(value))
            done = hid.at[w, cc, xx]
            got["h", w] = send([(done, done, dev(dx=dx)) for dx in (2, 1, 3)], hid.at[w, cc, pl.ds(0, NX - 1)])

        @task(f"c{w}")
        def _(w=w):
            got["h", w].wait_recv()
            got["c2", w] = send([(hid.at[w, cc], hid.at[w, cc], dev(other=True))], hid.at[w, cc])

        @task(f"d{w}")
        def _(w=w):
            got["c2", w].wait_recv()
            act = hid[w].reshape(2 * half, hpad)
            down = jnp.dot(act, wd[...], preferred_element_type=F32)
            pt[w] = down.astype(BF).reshape(4, NY, rows, feats)
            got["r1p", w] = send([(pt.at[w, n, :, :, A], r1p.at[w, n - 1], dev(dz=near[n])) for n in (1, 2, 3)], r1p.at[w])
            got["r1q", w] = send([(pt.at[w, :, j, :, B], r1q.at[w, j - 1], dev(dy=side[j])) for j in (1, 2, 3)], r1q.at[w])
            v = lax.dot_general(vv[...], act, NT, preferred_element_type=F32)
            rsc[w] = v[0:8]

        @task(f"e{w}")
        def _(w=w):
            got["r1p", w].wait_recv()
            v = pt[w, 0, :, :, A].astype(F32)
            for i in range(3):
                v = v + r1p[w, i].astype(F32)
            pt[w, 0, :, :, A] = v.astype(BF)
            got["r2p", w] = send([(pt.at[w, 0, j, :, A], r2p.at[w, j - 1], dev(dy=side[j])) for j in (1, 2, 3)], r2p.at[w])

        @task(f"f{w}")
        def _(w=w):
            got["r1q", w].wait_recv()
            v = pt[w, :, 0, :, B].astype(F32)
            for i in range(3):
                v = v + r1q[w, i].astype(F32)
            pt[w, :, 0, :, B] = v.astype(BF)
            got["r2q", w] = send([(pt.at[w, n, 0, :, B], r2q.at[w, n - 1], dev(dz=near[n])) for n in (1, 2, 3)], r2q.at[w])

        @task(f"g{w}")
        def _(w=w):
            got["r2p", w].wait_recv()
            got["r2q", w].wait_recv()
            a, b = pt[w, 0, 0, :, A].astype(F32), pt[w, 0, 0, :, B].astype(F32)
            for i in range(3):
                a, b = a + r2p[w, i].astype(F32), b + r2q[w, i].astype(F32)
            fs[w, :, A] = a.astype(BF)
            fs[w, :, B] = b.astype(BF)
            if w:
                got["rf", w] = send([(fs.at[w], rf.at[w - 1], dev(dz=FAR[w]))], rf.at[w - 1])

    bases = (0, len(tp_peers) + 1, len(tp_peers) + len(y_peers) + 2)

    def exchange(key, base, value, peers):
        sc[base] = value
        got[key] = send([(sc.at[base], sc.at[base + 1 + i], peer) for i, peer in enumerate(peers)],
                        sc.at[pl.ds(base + 1, len(peers))])

    def collect(key, base, peers):
        got[key].wait_recv()
        v = sc[base]
        for i in range(len(peers)):
            v = v + sc[base + 1 + i]
        return v

    keep = {}
    @task("v1")
    def _():
        owners()
        direct = lax.dot_general(sv3[...], x[0, pl.ds(0, 2)].reshape(half, feats), NT, preferred_element_type=F32)
        direct = jnp.where(lane < rows, direct[0:1] + direct[1:2] + direct[2:3], 0.0)
        cand = lax.broadcasted_iota(jnp.int32, (128, 128), 0).astype(F32)
        per = 128 // rows
        sums = jnp.zeros((16, 128), F32)
        for w in range(NW):
            for h in range(2):
                who = jnp.zeros((1, 128), F32)
                for p in range(per):
                    who = jnp.where(lane // rows == p, ow[w, 2 * h + p // NY, p % NY][0:1], who)
                score = rsc[w, :, pl.ds(h * 128, 128)]
                score = score[0:1] + score[1:2] + score[2:3]
                if w == 0 and h == 0:
                    score = score + direct
                terms = stacked(split(score, 3) + [jnp.ones((1, 128), BF)], 16)
                sums = sums + lax.dot_general(terms, jnp.where(cand == who, 1.0, 0.0).astype(BF), NT,
                                              preferred_element_type=F32)
        keep["count"] = sums[3:4]
        exchange("s1", bases[0], sums[0:1] + sums[1:2] + sums[2:3], tp_peers)

    @task("v2")
    def _():
        exchange("s2", bases[1], collect("s1", bases[0], tp_peers), y_peers)

    @task("v3")
    def _():
        exchange("s3", bases[2], collect("s2", bases[1], y_peers), z_peers)

    assert sorted(ORDER) == sorted(tasks)
    for name in ORDER:
        tasks[name]()

    v = fs[0].astype(F32)
    for w in range(1, NW):
        got["rf", w].wait_recv()
        v = v + rf[w - 1].astype(F32)
    out_ref[...] = v
    assert used[0] == ssem.shape[0]
    score_ref[...] = collect("s3", bases[2], z_peers) / keep["count"]
    for copy in flying:
        copy.wait_send()


def shards(preview, row_owner, norm_gain, w_gate, w_up, w_down, score_vec):
    rows, feats = preview.shape
    hidden = w_gate.shape[0]
    hpad = -(-hidden // 128) * 128
    half, blk, wide = 2 * NY * rows, 2 * NY * rows // NX, 2 * hidden
    pa = feats // 256 * 128
    pb = feats - pa
    sems = 61
    vmem = pl.BlockSpec(memory_space=pltpu.VMEM)
    hbm = pl.BlockSpec(memory_space=pl.ANY)
    verified, scores = pl.pallas_call(
        functools.partial(kernel, pa),
        out_shape=(jax.ShapeDtypeStruct((rows, feats), F32), jax.ShapeDtypeStruct((1, 128), F32)),
        in_specs=[hbm, pl.BlockSpec(memory_space=pltpu.SMEM), hbm, hbm, hbm, hbm, hbm],
        out_specs=(vmem, vmem),
        scratch_shapes=[
            pltpu.VMEM((rows, feats), BF),
            pltpu.VMEM((1, feats), F32),
            pltpu.VMEM((1, feats), F32),
            pltpu.VMEM((NW, 4, NY, rows, feats), BF),
            pltpu.VMEM((2 * hidden, feats), BF),
            pltpu.VMEM((feats, 2 * hidden), BF),
            pltpu.VMEM((hpad, feats), BF),
            pltpu.VMEM((16, hpad), BF),
            pltpu.VMEM((16, feats), BF),
            pltpu.VMEM((2 * NX, 1, 128), F32),
            pltpu.VMEM((NW, half, wide), BF),
            pltpu.VMEM((NW, NX, blk, wide), F32),
            pltpu.VMEM((NW, NX, blk, wide), BF),
            pltpu.VMEM((NW, half, wide), BF),
            pltpu.VMEM((NW, NX - 1, blk, wide), BF),
            pltpu.VMEM((NW, 2, NX, blk, hpad), BF),
            pltpu.VMEM((NW, 4, NY, rows, feats), BF),
            pltpu.VMEM((NW, 3, NY, rows, pa), BF),
            pltpu.VMEM((NW, 3, 4, rows, pb), BF),
            pltpu.VMEM((NW, 3, rows, pa), BF),
            pltpu.VMEM((NW, 3, rows, pb), BF),
            pltpu.VMEM((NW, rows, feats), BF),
            pltpu.VMEM((NW - 1, rows, feats), BF),
            pltpu.VMEM((NW, 4, NY, 2, 128), F32),
            pltpu.VMEM((NW, 8, 2 * half), F32),
            pltpu.VMEM((2 * NX + NY + NZ, 1, 128), F32),
            pltpu.SemaphoreType.DMA((8,)),
            pltpu.SemaphoreType.DMA((sems,)),
            pltpu.SemaphoreType.DMA((sems,)),
        ],
        compiler_params=pltpu.CompilerParams(
            collective_id=0, has_side_effects=True, vmem_limit_bytes=56 << 20),
    )(preview, row_owner, norm_gain[None, :], w_gate, w_up, w_down, score_vec[None, :])
    return (verified + preview.astype(F32)).astype(BF), scores[0, :CAND]


def solution(mesh):
    placed = (
        P("section", "tp"),
        P("section"),
        P("tp"),
        P("section", "tp"),
        P("section", "tp"),
        P("section", "tp"),
        P("tp"),
    )
    return jax.shard_map(
        shards, mesh=mesh, in_specs=placed, out_specs=(P("section", "tp"), P()), check_vma=False
    )
```

```python
import functools

import jax
import jax.numpy as jnp
from jax import lax
from jax.experimental import pallas as pl
from jax.experimental.pallas import tpu as pltpu
from jax.sharding import PartitionSpec as P

CAND = 32
NX, NY, NZ = 4, 4, 16
NW = 4
EPS = 1e-05
BF = jnp.bfloat16
F32 = jnp.float32
FAR = (0, 4, -4, 8)
NT = (((1,), (1,)), ((), ()))
MESH = pl.DeviceIdType.MESH
ORDER = (
    "far2", "nq", "wts", "far3", "s0", "far1", "nrm", "s2", "p0", "q0", "s1", "s3",
    "q2", "vec", "p2", "own2", "m0", "q3", "q1", "p3", "x0", "m2", "own3", "p1",
    "x2", "m3", "h0", "x3", "m1", "h2", "c0", "x1", "h3", "d0", "c2", "d2",
    "h1", "c3", "d3", "c1", "f2", "d1", "v1", "f3", "e3", "f0", "e2", "v2",
    "f1", "g3", "e1", "e0", "v3", "g2", "g1", "g0",
)


def split(v, parts):
    out = []
    for _ in range(parts):
        term = v.astype(BF)
        out.append(term)
        v = v - term.astype(F32)
    return out


def stacked(terms, rows):
    width = terms[0].shape[1]
    sub = lax.broadcasted_iota(jnp.int32, (rows, width), 0)
    out = jnp.zeros((rows, width), F32)
    for i, term in enumerate(terms):
        out = jnp.where(sub == i, term.astype(F32), out)
    return out.astype(BF)


def kernel(pa, prev_hbm, owner_ref, gain_hbm, wg_ref, wu_ref, wd_ref, sv_hbm, out_ref, score_ref,
           prev_ref, gain_ref, sv_ref, x, wgu, wt, wd, vv, sv3, nq, gus, guo, gub, rc, rx, hid, pt, r1p, r1q, r2p, r2q, fs, rf, ow, rsc, sc,
           lsem, ssem, rsem):
    rows, feats, hidden = prev_hbm.shape[0], prev_hbm.shape[1], wg_ref.shape[0]
    hpad = -(-hidden // 128) * 128
    full = hidden // 128 * 128
    rest = hidden - full
    width = 2 * hidden
    half, blk = 2 * NY * rows, 2 * NY * rows // NX
    A, B = pl.ds(0, pa), pl.ds(pa, feats - pa)
    s, t = lax.axis_index("section"), lax.axis_index("tp")
    yy, zz = s // NZ, s % NZ
    xx, cc = t // 2, t % 2
    near = (0, -1, 1, 2 * (1 - 2 * (zz % 2)))
    side = (0, -1, 1, 2)

    def dev(dx=0, dy=0, dz=0, other=False):
        core = 1 - cc if other else cc
        return (((yy + dy + NY) % NY) * NZ + (zz + dz + NZ) % NZ, ((xx + dx) % NX) * 2 + core)

    used = [0]
    kinds = {}
    flying = []

    def send(items, union, kind=None):
        i = used[0]
        used[0] += 1
        k = kinds.setdefault(kind or i, len(kinds))
        for src, dst, to in items:
            pltpu.make_async_remote_copy(src_ref=src, dst_ref=dst, send_sem=ssem.at[k], recv_sem=rsem.at[i],
                                         device_id=to, device_id_type=MESH).start()
        whole = pltpu.make_async_remote_copy(src_ref=union, dst_ref=union, send_sem=ssem.at[k], recv_sem=rsem.at[i],
                                             device_id=items[0][2], device_id_type=MESH)
        if kind is None:
            flying.append(whole)
        return whole

    tp_peers = [dev(dx=dx, other=o) for dx in range(NX) for o in (False, True) if (dx, o) != (0, False)]
    y_peers = [dev(dy=dy) for dy in range(1, NY)]
    z_peers = [dev(dz=dz) for dz in range(1, NZ)]
    barrier = pltpu.get_barrier_semaphore()
    for peer in z_peers + y_peers + tp_peers:
        pl.semaphore_signal(barrier, inc=1, device_id=peer, device_id_type=MESH)
    loads = []

    def load(src, dst):
        copy = pltpu.make_async_copy(src, dst, lsem.at[len(loads)])
        copy.start()
        loads.append(copy)

    load(prev_hbm, prev_ref)
    load(gain_hbm, gain_ref)
    load(sv_hbm, sv_ref)
    if full:
        load(wg_ref.at[pl.ds(0, full)], wgu.at[pl.ds(0, full)])
        load(wu_ref.at[pl.ds(0, full)], wgu.at[pl.ds(full, full)])
    if rest:
        load(wg_ref.at[pl.ds(full, rest)], wgu.at[pl.ds(2 * full, rest)])
        load(wu_ref.at[pl.ds(full, rest)], wgu.at[pl.ds(2 * full + rest, rest)])
    load(wd_ref, wd.at[pl.ds(0, hidden)])
    if rest:
        wd[pl.ds(hidden, hpad - hidden), :] = jnp.zeros((hpad - hidden, feats), BF)
    loads[0].wait()
    x[0, 0, 0] = prev_ref[...]
    lane = lax.broadcasted_iota(jnp.int32, (1, 128), 1)
    owner = jnp.zeros((1, 128), F32)
    for r in range(rows):
        owner = jnp.where(lane % rows == r, owner_ref[r].astype(F32), owner)
    own = prev_ref[...].astype(F32)
    sq = jnp.sum(own * own, axis=1, keepdims=True)
    eye = (lax.broadcasted_iota(jnp.int32, (rows, 128), 1) % rows
           == lax.broadcasted_iota(jnp.int32, (rows, 128), 0))
    nq[0] = jnp.sum(jnp.where(eye, sq, 0.0), axis=0, keepdims=True)
    pl.semaphore_wait(barrier, len(tp_peers + y_peers + z_peers))

    got = {}
    tasks = {}

    def task(name):
        def add(fn):
            tasks[name] = fn
            return fn
        return add

    def spread(w):
        got["p2", w] = send([(x.at[w, 0, 0, :, A], x.at[w, 0, j, :, A], dev(dy=-side[j])) for j in (1, 2, 3)],
                            x.at[w, 0, pl.ds(1, 3), :, A], "p2")
        got["q2", w] = send([(x.at[w, 0, 0, :, B], x.at[w, n, 0, :, B], dev(dz=-near[n])) for n in (1, 2, 3)],
                            x.at[w, pl.ds(1, 3), 0, :, B], "q2")

    for w in range(NW):
        if w:
            @task(f"far{w}")
            def _(w=w):
                got["far", w] = send([(x.at[0, 0, 0], x.at[w, 0, 0], dev(dz=-FAR[w]))], x.at[w, 0, 0], "far")

        @task(f"s{w}")
        def _(w=w):
            if w:
                got["far", w].wait_recv()
            spread(w)

        @task(f"p{w}")
        def _(w=w):
            got["p2", w].wait_recv()
            got["p3", w] = send([(x.at[w, 0, :, :, A], x.at[w, n, :, :, A], dev(dz=-near[n])) for n in (1, 2, 3)],
                                x.at[w, pl.ds(1, 3), :, :, A], "p3")

        @task(f"q{w}")
        def _(w=w):
            got["q2", w].wait_recv()
            got["q3", w] = send([(x.at[w, :, 0, :, B], x.at[w, :, j, :, B], dev(dy=-side[j])) for j in (1, 2, 3)],
                                x.at[w, :, pl.ds(1, 3), :, B], "q3")

    @task("nq")
    def _():
        got["nq"] = send([(nq.at[0], nq.at[i + 1], peer) for i, peer in enumerate(tp_peers)],
                         nq.at[pl.ds(1, len(tp_peers))])

    @task("nrm")
    def _():
        got["nq"].wait_recv()
        total = nq[0]
        for i in range(len(tp_peers)):
            total = total + nq[i + 1]
        ow[0, 0, 0, 0:1] = owner
        ow[0, 0, 0, 1:2] = lax.rsqrt(total / (feats * NX * 2) + EPS)
        got["o1"] = send([(ow.at[0, 0, 0], ow.at[w, 0, 0], dev(dz=-FAR[w])) for w in (1, 2, 3)],
                         ow.at[pl.ds(1, 3), 0, 0])

    @task("own2")
    def _():
        got["o1"].wait_recv()
        got["o2"] = send([(ow.at[:, 0, 0], ow.at[:, 0, j], dev(dy=-side[j])) for j in (1, 2, 3)],
                         ow.at[:, 0, pl.ds(1, 3)])

    @task("own3")
    def _():
        got["o2"].wait_recv()
        got["o3"] = send([(ow.at[:, 0], ow.at[:, n], dev(dz=-near[n])) for n in (1, 2, 3)], ow.at[:, pl.ds(1, 3)])

    have = []

    def owners():
        if not have:
            got["o3"].wait_recv()
            have.append(True)

    step = 128

    @task("wts")
    def _():
        for copy in loads[1:]:
            copy.wait()
        for i in range(width // step):
            piece = wgu[pl.ds(i * step, step), :].astype(F32) * gain_ref[...]
            wt[:, pl.ds(i * step, step)] = piece.astype(BF).T

    @task("vec")
    def _():
        sv3[...] = stacked(split(sv_ref[...], 3), 16)
        v = lax.dot_general(sv3[...], wd[...], NT, preferred_element_type=F32)
        vv[...] = stacked(split(v[0:1] + v[1:2] + v[2:3], 3), 16)

    def product(w, core):
        part = x[w, pl.ds(2 * core, 2)].reshape(half, feats)
        return jnp.dot(part, wt[...], preferred_element_type=F32)

    for w in range(NW):
        @task(f"m{w}")
        def _(w=w):
            got["p3", w].wait_recv()
            got["q3", w].wait_recv()
            gus[w] = product(w, 1 - cc).astype(BF)
            got["c1", w] = send([(gus.at[w], rc.at[w], dev(other=True))], rc.at[w], "c1")
            guo[w] = product(w, cc).reshape(NX, blk, width)

        @task(f"x{w}")
        def _(w=w):
            got["c1", w].wait_recv()
            total = guo[w] + rc[w].astype(F32).reshape(NX, blk, width)
            guo[w] = total
            gub[w] = total.astype(BF)
            got["x", w] = send([(gub.at[w, (xx + dx) % NX], rx.at[w, dx - 1], dev(dx=dx)) for dx in (2, 1, 3)], rx.at[w], "x")

        @task(f"h{w}")
        def _(w=w):
            owners()
            got["x", w].wait_recv()
            gu = guo[w, xx]
            for i in range(NX - 1):
                gu = gu + rx[w, i].astype(F32)
            scales = [ow[w, 2 * cc + xx // 2, 2 * (xx % 2) + i][1:2] for i in range(2)]
            scale = jnp.concatenate([jnp.sum(jnp.where(eye & (lane < rows), sc_, 0.0), axis=1, keepdims=True)
                                     for sc_ in scales], axis=0)
            gu = gu * scale

            def act(gate, up):
                return (gate / (1.0 + jnp.exp(-gate)) * up).astype(BF)

            if full:
                hid[w, cc, xx, :, pl.ds(0, full)] = act(gu[:, 0:full], gu[:, full:2 * full])
            if rest:
                last = gu[:, 2 * full:]
                at_lane = lax.broadcasted_iota(jnp.int32, last.shape, 1)
                value = act(last, pltpu.roll(last, 128 - rest, 1))
                hid[w, cc, xx, :, pl.ds(full, 128)] = jnp.where(at_lane < rest, value, jnp.zeros_like(value))
            done = hid.at[w, cc, xx]
            got["h", w] = send([(done, done, dev(dx=dx)) for dx in (2, 1, 3)], hid.at[w, cc, pl.ds(0, NX - 1)], "h")

        @task(f"c{w}")
        def _(w=w):
            got["h", w].wait_recv()
            got["c2", w] = send([(hid.at[w, cc], hid.at[w, cc], dev(other=True))], hid.at[w, cc], "c2")

        @task(f"d{w}")
        def _(w=w):
            got["c2", w].wait_recv()
            act = hid[w].reshape(2 * half, hpad)
            down = jnp.dot(act, wd[...], preferred_element_type=F32)
            pt[w] = down.astype(BF).reshape(4, NY, rows, feats)
            got["r1p", w] = send([(pt.at[w, n, :, :, A], r1p.at[w, n - 1], dev(dz=near[n])) for n in (1, 2, 3)], r1p.at[w], "r1p")
            got["r1q", w] = send([(pt.at[w, :, j, :, B], r1q.at[w, j - 1], dev(dy=side[j])) for j in (1, 2, 3)], r1q.at[w], "r1q")
            v = lax.dot_general(vv[...], act, NT, preferred_element_type=F32)
            rsc[w] = v[0:8]

        @task(f"e{w}")
        def _(w=w):
            got["r1p", w].wait_recv()
            v = pt[w, 0, :, :, A].astype(F32)
            for i in range(3):
                v = v + r1p[w, i].astype(F32)
            pt[w, 0, :, :, A] = v.astype(BF)
            got["r2p", w] = send([(pt.at[w, 0, j, :, A], r2p.at[w, j - 1], dev(dy=side[j])) for j in (1, 2, 3)], r2p.at[w], "r2p")

        @task(f"f{w}")
        def _(w=w):
            got["r1q", w].wait_recv()
            v = pt[w, :, 0, :, B].astype(F32)
            for i in range(3):
                v = v + r1q[w, i].astype(F32)
            pt[w, :, 0, :, B] = v.astype(BF)
            got["r2q", w] = send([(pt.at[w, n, 0, :, B], r2q.at[w, n - 1], dev(dz=near[n])) for n in (1, 2, 3)], r2q.at[w], "r2q")

        @task(f"g{w}")
        def _(w=w):
            got["r2p", w].wait_recv()
            got["r2q", w].wait_recv()
            a, b = pt[w, 0, 0, :, A].astype(F32), pt[w, 0, 0, :, B].astype(F32)
            for i in range(3):
                a, b = a + r2p[w, i].astype(F32), b + r2q[w, i].astype(F32)
            fs[w, :, A] = a.astype(BF)
            fs[w, :, B] = b.astype(BF)
            if w:
                got["rf", w] = send([(fs.at[w], rf.at[w - 1], dev(dz=FAR[w]))], rf.at[w - 1], "rf")

    bases = (0, len(tp_peers) + 1, len(tp_peers) + len(y_peers) + 2)

    def exchange(key, base, value, peers):
        sc[base] = value
        got[key] = send([(sc.at[base], sc.at[base + 1 + i], peer) for i, peer in enumerate(peers)],
                        sc.at[pl.ds(base + 1, len(peers))])

    def collect(key, base, peers):
        got[key].wait_recv()
        v = sc[base]
        for i in range(len(peers)):
            v = v + sc[base + 1 + i]
        return v

    keep = {}
    @task("v1")
    def _():
        owners()
        direct = lax.dot_general(sv3[...], x[0, pl.ds(0, 2)].reshape(half, feats), NT, preferred_element_type=F32)
        direct = jnp.where(lane < rows, direct[0:1] + direct[1:2] + direct[2:3], 0.0)
        cand = lax.broadcasted_iota(jnp.int32, (128, 128), 0).astype(F32)
        per = 128 // rows
        sums = jnp.zeros((16, 128), F32)
        for w in range(NW):
            for h in range(2):
                who = jnp.zeros((1, 128), F32)
                for p in range(per):
                    who = jnp.where(lane // rows == p, ow[w, 2 * h + p // NY, p % NY][0:1], who)
                score = rsc[w, :, pl.ds(h * 128, 128)]
                score = score[0:1] + score[1:2] + score[2:3]
                if w == 0 and h == 0:
                    score = score + direct
                terms = stacked(split(score, 3) + [jnp.ones((1, 128), BF)], 16)
                sums = sums + lax.dot_general(terms, jnp.where(cand == who, 1.0, 0.0).astype(BF), NT,
                                              preferred_element_type=F32)
        keep["count"] = sums[3:4]
        exchange("s1", bases[0], sums[0:1] + sums[1:2] + sums[2:3], tp_peers)

    @task("v2")
    def _():
        exchange("s2", bases[1], collect("s1", bases[0], tp_peers), y_peers)

    @task("v3")
    def _():
        exchange("s3", bases[2], collect("s2", bases[1], y_peers), z_peers)

    assert sorted(ORDER) == sorted(tasks)
    for name in ORDER:
        tasks[name]()

    v = fs[0].astype(F32)
    for w in range(1, NW):
        got["rf", w].wait_recv()
        v = v + rf[w - 1].astype(F32)
    out_ref[...] = v
    assert (used[0], len(kinds)) == (rsem.shape[0], ssem.shape[0])
    score_ref[...] = collect("s3", bases[2], z_peers) / keep["count"]
    for copy in flying:
        copy.wait_send()
    later = pl.ds(1, NW - 1)
    every = {
        "far": x.at[later, 0, 0], "p2": x.at[:, 0, pl.ds(1, 3), :, A], "q2": x.at[:, pl.ds(1, 3), 0, :, B],
        "p3": x.at[:, pl.ds(1, 3), :, :, A], "q3": x.at[:, :, pl.ds(1, 3), :, B], "c1": rc, "x": rx,
        "h": hid.at[:, cc, pl.ds(0, NX - 1)], "c2": hid.at[:, cc], "r1p": r1p, "r1q": r1q, "r2p": r2p, "r2q": r2q,
        "rf": rf,
    }
    for kind, union in every.items():
        pltpu.make_async_remote_copy(src_ref=union, dst_ref=union, send_sem=ssem.at[kinds[kind]], recv_sem=rsem.at[0],
                                     device_id=tp_peers[0], device_id_type=MESH).wait_send()


def shards(preview, row_owner, norm_gain, w_gate, w_up, w_down, score_vec):
    rows, feats = preview.shape
    hidden = w_gate.shape[0]
    hpad = -(-hidden // 128) * 128
    half, blk, wide = 2 * NY * rows, 2 * NY * rows // NX, 2 * hidden
    pa = feats // 256 * 128
    pb = feats - pa
    sems, kinds = 61, 21
    vmem = pl.BlockSpec(memory_space=pltpu.VMEM)
    hbm = pl.BlockSpec(memory_space=pl.ANY)
    verified, scores = pl.pallas_call(
        functools.partial(kernel, pa),
        out_shape=(jax.ShapeDtypeStruct((rows, feats), F32), jax.ShapeDtypeStruct((1, 128), F32)),
        in_specs=[hbm, pl.BlockSpec(memory_space=pltpu.SMEM), hbm, hbm, hbm, hbm, hbm],
        out_specs=(vmem, vmem),
        scratch_shapes=[
            pltpu.VMEM((rows, feats), BF),
            pltpu.VMEM((1, feats), F32),
            pltpu.VMEM((1, feats), F32),
            pltpu.VMEM((NW, 4, NY, rows, feats), BF),
            pltpu.VMEM((2 * hidden, feats), BF),
            pltpu.VMEM((feats, 2 * hidden), BF),
            pltpu.VMEM((hpad, feats), BF),
            pltpu.VMEM((16, hpad), BF),
            pltpu.VMEM((16, feats), BF),
            pltpu.VMEM((2 * NX, 1, 128), F32),
            pltpu.VMEM((NW, half, wide), BF),
            pltpu.VMEM((NW, NX, blk, wide), F32),
            pltpu.VMEM((NW, NX, blk, wide), BF),
            pltpu.VMEM((NW, half, wide), BF),
            pltpu.VMEM((NW, NX - 1, blk, wide), BF),
            pltpu.VMEM((NW, 2, NX, blk, hpad), BF),
            pltpu.VMEM((NW, 4, NY, rows, feats), BF),
            pltpu.VMEM((NW, 3, NY, rows, pa), BF),
            pltpu.VMEM((NW, 3, 4, rows, pb), BF),
            pltpu.VMEM((NW, 3, rows, pa), BF),
            pltpu.VMEM((NW, 3, rows, pb), BF),
            pltpu.VMEM((NW, rows, feats), BF),
            pltpu.VMEM((NW - 1, rows, feats), BF),
            pltpu.VMEM((NW, 4, NY, 2, 128), F32),
            pltpu.VMEM((NW, 8, 2 * half), F32),
            pltpu.VMEM((2 * NX + NY + NZ, 1, 128), F32),
            pltpu.SemaphoreType.DMA((8,)),
            pltpu.SemaphoreType.DMA((kinds,)),
            pltpu.SemaphoreType.DMA((sems,)),
        ],
        compiler_params=pltpu.CompilerParams(
            collective_id=0, has_side_effects=True, vmem_limit_bytes=56 << 20),
    )(preview, row_owner, norm_gain[None, :], w_gate, w_up, w_down, score_vec[None, :])
    return (verified + preview.astype(F32)).astype(BF), scores[0, :CAND]


def solution(mesh):
    placed = (
        P("section", "tp"),
        P("section"),
        P("tp"),
        P("section", "tp"),
        P("section", "tp"),
        P("section", "tp"),
        P("tp"),
    )
    return jax.shard_map(
        shards, mesh=mesh, in_specs=placed, out_specs=(P("section", "tp"), P()), check_vma=False
    )
```

```python
import functools

import jax
import jax.numpy as jnp
from jax import lax
from jax.experimental import pallas as pl
from jax.experimental.pallas import tpu as pltpu
from jax.sharding import PartitionSpec as P

CAND = 32
NX, NY, NZ = 4, 4, 16
NW = 4
EPS = 1e-05
BF = jnp.bfloat16
F32 = jnp.float32
FAR = (0, 4, -4, 8)
NT = (((1,), (1,)), ((), ()))
MESH = pl.DeviceIdType.MESH
ORDER = (
    "far2", "nq", "wts", "far3", "s0", "far1", "nrm", "s2", "p0", "q0", "s1", "s3",
    "q2", "vec", "p2", "own2", "m0", "q3", "q1", "p3", "x0", "m2", "own3", "p1",
    "x2", "m3", "h0", "x3", "m1", "h2", "c0", "x1", "h3", "d0", "c2", "d2",
    "h1", "c3", "d3", "c1", "f2", "d1", "v1", "f3", "e3", "f0", "e2", "v2",
    "f1", "g3", "e1", "e0", "v3", "g2", "g1", "g0",
)


def split(v, parts):
    out = []
    for _ in range(parts):
        term = v.astype(BF)
        out.append(term)
        v = v - term.astype(F32)
    return out


def stacked(terms, rows):
    width = terms[0].shape[1]
    sub = lax.broadcasted_iota(jnp.int32, (rows, width), 0)
    out = jnp.zeros((rows, width), F32)
    for i, term in enumerate(terms):
        out = jnp.where(sub == i, term.astype(F32), out)
    return out.astype(BF)


def kernel(pa, prev_hbm, owner_ref, gain_hbm, wg_ref, wu_ref, wd_ref, sv_hbm, out_ref, score_ref,
           prev_ref, gain_ref, sv_ref, x, wgu, wt, wd, vv, sv3, nq, gus, guo, gub, rc, rx, hid, pt, r1p, r1q, r2p, r2q, fs, rf, ow, rsc, sc,
           lsem, ssem, rsem):
    rows, feats, hidden = prev_hbm.shape[0], prev_hbm.shape[1], wg_ref.shape[0]
    hpad = -(-hidden // 128) * 128
    full = hidden // 128 * 128
    rest = hidden - full
    width = 2 * hidden
    half, blk = 2 * NY * rows, 2 * NY * rows // NX
    A, B = pl.ds(0, pa), pl.ds(pa, feats - pa)
    s, t = lax.axis_index("section"), lax.axis_index("tp")
    yy, zz = s // NZ, s % NZ
    xx, cc = t // 2, t % 2
    near = (0, -1, 1, 2 * (1 - 2 * (zz % 2)))
    side = (0, -1, 1, 2)

    def dev(dx=0, dy=0, dz=0, other=False):
        core = 1 - cc if other else cc
        return (((yy + dy + NY) % NY) * NZ + (zz + dz + NZ) % NZ, ((xx + dx) % NX) * 2 + core)

    used = [0]
    kinds = {}
    flying = []

    def send(items, union, kind=None):
        i = used[0]
        used[0] += 1
        k = kinds.setdefault(kind or i, len(kinds))
        for src, dst, to in items:
            pltpu.make_async_remote_copy(src_ref=src, dst_ref=dst, send_sem=ssem.at[k], recv_sem=rsem.at[i],
                                         device_id=to, device_id_type=MESH).start()
        whole = pltpu.make_async_remote_copy(src_ref=union, dst_ref=union, send_sem=ssem.at[k], recv_sem=rsem.at[i],
                                             device_id=items[0][2], device_id_type=MESH)
        if kind is None:
            flying.append(whole)
        return whole

    tp_peers = [dev(dx=dx, other=o) for dx in range(NX) for o in (False, True) if (dx, o) != (0, False)]
    y_peers = [dev(dy=dy) for dy in range(1, NY)]
    z_peers = [dev(dz=dz) for dz in range(1, NZ)]
    barrier = pltpu.get_barrier_semaphore()
    for peer in z_peers + y_peers + tp_peers:
        pl.semaphore_signal(barrier, inc=1, device_id=peer, device_id_type=MESH)
    loads = []

    def load(src, dst):
        copy = pltpu.make_async_copy(src, dst, lsem.at[len(loads)])
        copy.start()
        loads.append(copy)

    load(prev_hbm, prev_ref)
    load(gain_hbm, gain_ref)
    load(sv_hbm, sv_ref)
    if full:
        load(wg_ref.at[pl.ds(0, full)], wgu.at[pl.ds(0, full)])
        load(wu_ref.at[pl.ds(0, full)], wgu.at[pl.ds(full, full)])
    if rest:
        load(wg_ref.at[pl.ds(full, rest)], wgu.at[pl.ds(2 * full, rest)])
        load(wu_ref.at[pl.ds(full, rest)], wgu.at[pl.ds(2 * full + rest, rest)])
    load(wd_ref, wd.at[pl.ds(0, hidden)])
    if rest:
        wd[pl.ds(hidden, hpad - hidden), :] = jnp.zeros((hpad - hidden, feats), BF)
    loads[0].wait()
    x[0, 0, 0] = prev_ref[...]
    lane = lax.broadcasted_iota(jnp.int32, (1, 128), 1)
    owner = jnp.zeros((1, 128), F32)
    for r in range(rows):
        owner = jnp.where(lane % rows == r, owner_ref[r].astype(F32), owner)
    own = prev_ref[...].astype(F32)
    sq = jnp.sum(own * own, axis=1, keepdims=True)
    eye = (lax.broadcasted_iota(jnp.int32, (rows, 128), 1) % rows
           == lax.broadcasted_iota(jnp.int32, (rows, 128), 0))
    nq[0] = jnp.sum(jnp.where(eye, sq, 0.0), axis=0, keepdims=True)

    got = {}
    tasks = {}

    def task(name):
        def add(fn):
            tasks[name] = fn
            return fn
        return add

    def spread(w):
        got["p2", w] = send([(x.at[w, 0, 0, :, A], x.at[w, 0, j, :, A], dev(dy=-side[j])) for j in (1, 2, 3)],
                            x.at[w, 0, pl.ds(1, 3), :, A], "p2")
        got["q2", w] = send([(x.at[w, 0, 0, :, B], x.at[w, n, 0, :, B], dev(dz=-near[n])) for n in (1, 2, 3)],
                            x.at[w, pl.ds(1, 3), 0, :, B], "q2")

    for w in range(NW):
        if w:
            @task(f"far{w}")
            def _(w=w):
                got["far", w] = send([(x.at[0, 0, 0], x.at[w, 0, 0], dev(dz=-FAR[w]))], x.at[w, 0, 0], "far")

        @task(f"s{w}")
        def _(w=w):
            if w:
                got["far", w].wait_recv()
            spread(w)

        @task(f"p{w}")
        def _(w=w):
            got["p2", w].wait_recv()
            got["p3", w] = send([(x.at[w, 0, :, :, A], x.at[w, n, :, :, A], dev(dz=-near[n])) for n in (1, 2, 3)],
                                x.at[w, pl.ds(1, 3), :, :, A], "p3")

        @task(f"q{w}")
        def _(w=w):
            got["q2", w].wait_recv()
            got["q3", w] = send([(x.at[w, :, 0, :, B], x.at[w, :, j, :, B], dev(dy=-side[j])) for j in (1, 2, 3)],
                                x.at[w, :, pl.ds(1, 3), :, B], "q3")

    @task("nq")
    def _():
        got["nq"] = send([(nq.at[0], nq.at[i + 1], peer) for i, peer in enumerate(tp_peers)],
                         nq.at[pl.ds(1, len(tp_peers))])

    @task("nrm")
    def _():
        got["nq"].wait_recv()
        total = nq[0]
        for i in range(len(tp_peers)):
            total = total + nq[i + 1]
        ow[0, 0, 0, 0:1] = owner
        ow[0, 0, 0, 1:2] = lax.rsqrt(total / (feats * NX * 2) + EPS)
        got["o1"] = send([(ow.at[0, 0, 0], ow.at[w, 0, 0], dev(dz=-FAR[w])) for w in (1, 2, 3)],
                         ow.at[pl.ds(1, 3), 0, 0])

    @task("own2")
    def _():
        got["o1"].wait_recv()
        got["o2"] = send([(ow.at[:, 0, 0], ow.at[:, 0, j], dev(dy=-side[j])) for j in (1, 2, 3)],
                         ow.at[:, 0, pl.ds(1, 3)])

    @task("own3")
    def _():
        got["o2"].wait_recv()
        got["o3"] = send([(ow.at[:, 0], ow.at[:, n], dev(dz=-near[n])) for n in (1, 2, 3)], ow.at[:, pl.ds(1, 3)])

    have = []

    def owners():
        if not have:
            got["o3"].wait_recv()
            have.append(True)

    step = 128

    @task("wts")
    def _():
        for copy in loads[1:]:
            copy.wait()
        for i in range(width // step):
            piece = wgu[pl.ds(i * step, step), :].astype(F32) * gain_ref[...]
            wt[:, pl.ds(i * step, step)] = piece.astype(BF).T

    @task("vec")
    def _():
        sv3[...] = stacked(split(sv_ref[...], 3), 16)
        v = lax.dot_general(sv3[...], wd[...], NT, preferred_element_type=F32)
        vv[...] = stacked(split(v[0:1] + v[1:2] + v[2:3], 3), 16)

    def product(w, core):
        part = x[w, pl.ds(2 * core, 2)].reshape(half, feats)
        return jnp.dot(part, wt[...], preferred_element_type=F32)

    for w in range(NW):
        @task(f"m{w}")
        def _(w=w):
            got["p3", w].wait_recv()
            got["q3", w].wait_recv()
            gus[w] = product(w, 1 - cc).astype(BF)
            got["c1", w] = send([(gus.at[w], rc.at[w], dev(other=True))], rc.at[w], "c1")
            guo[w] = product(w, cc).reshape(NX, blk, width)

        @task(f"x{w}")
        def _(w=w):
            got["c1", w].wait_recv()
            total = guo[w] + rc[w].astype(F32).reshape(NX, blk, width)
            guo[w] = total
            gub[w] = total.astype(BF)
            got["x", w] = send([(gub.at[w, (xx + dx) % NX], rx.at[w, dx - 1], dev(dx=dx)) for dx in (2, 1, 3)], rx.at[w], "x")

        @task(f"h{w}")
        def _(w=w):
            owners()
            got["x", w].wait_recv()
            gu = guo[w, xx]
            for i in range(NX - 1):
                gu = gu + rx[w, i].astype(F32)
            scales = [ow[w, 2 * cc + xx // 2, 2 * (xx % 2) + i][1:2] for i in range(2)]
            scale = jnp.concatenate([jnp.sum(jnp.where(eye & (lane < rows), sc_, 0.0), axis=1, keepdims=True)
                                     for sc_ in scales], axis=0)
            gu = gu * scale

            def act(gate, up):
                return (gate / (1.0 + jnp.exp(-gate)) * up).astype(BF)

            if full:
                hid[w, cc, xx, :, pl.ds(0, full)] = act(gu[:, 0:full], gu[:, full:2 * full])
            if rest:
                last = gu[:, 2 * full:]
                at_lane = lax.broadcasted_iota(jnp.int32, last.shape, 1)
                value = act(last, pltpu.roll(last, 128 - rest, 1))
                hid[w, cc, xx, :, pl.ds(full, 128)] = jnp.where(at_lane < rest, value, jnp.zeros_like(value))
            done = hid.at[w, cc, xx]
            got["h", w] = send([(done, done, dev(dx=dx)) for dx in (2, 1, 3)], hid.at[w, cc, pl.ds(0, NX - 1)], "h")

        @task(f"c{w}")
        def _(w=w):
            got["h", w].wait_recv()
            got["c2", w] = send([(hid.at[w, cc], hid.at[w, cc], dev(other=True))], hid.at[w, cc], "c2")

        @task(f"d{w}")
        def _(w=w):
            got["c2", w].wait_recv()
            act = hid[w].reshape(2 * half, hpad)
            down = jnp.dot(act, wd[...], preferred_element_type=F32)
            pt[w] = down.astype(BF).reshape(4, NY, rows, feats)
            got["r1p", w] = send([(pt.at[w, n, :, :, A], r1p.at[w, n - 1], dev(dz=near[n])) for n in (1, 2, 3)], r1p.at[w], "r1p")
            got["r1q", w] = send([(pt.at[w, :, j, :, B], r1q.at[w, j - 1], dev(dy=side[j])) for j in (1, 2, 3)], r1q.at[w], "r1q")
            v = lax.dot_general(vv[...], act, NT, preferred_element_type=F32)
            rsc[w] = v[0:8]

        @task(f"e{w}")
        def _(w=w):
            got["r1p", w].wait_recv()
            v = pt[w, 0, :, :, A].astype(F32)
            for i in range(3):
                v = v + r1p[w, i].astype(F32)
            pt[w, 0, :, :, A] = v.astype(BF)
            got["r2p", w] = send([(pt.at[w, 0, j, :, A], r2p.at[w, j - 1], dev(dy=side[j])) for j in (1, 2, 3)], r2p.at[w], "r2p")

        @task(f"f{w}")
        def _(w=w):
            got["r1q", w].wait_recv()
            v = pt[w, :, 0, :, B].astype(F32)
            for i in range(3):
                v = v + r1q[w, i].astype(F32)
            pt[w, :, 0, :, B] = v.astype(BF)
            got["r2q", w] = send([(pt.at[w, n, 0, :, B], r2q.at[w, n - 1], dev(dz=near[n])) for n in (1, 2, 3)], r2q.at[w], "r2q")

        @task(f"g{w}")
        def _(w=w):
            got["r2p", w].wait_recv()
            got["r2q", w].wait_recv()
            a, b = pt[w, 0, 0, :, A].astype(F32), pt[w, 0, 0, :, B].astype(F32)
            for i in range(3):
                a, b = a + r2p[w, i].astype(F32), b + r2q[w, i].astype(F32)
            fs[w, :, A] = a.astype(BF)
            fs[w, :, B] = b.astype(BF)
            if w:
                got["rf", w] = send([(fs.at[w], rf.at[w - 1], dev(dz=FAR[w]))], rf.at[w - 1], "rf")

    bases = (0, len(tp_peers) + 1, len(tp_peers) + len(y_peers) + 2)

    def exchange(key, base, value, peers):
        sc[base] = value
        got[key] = send([(sc.at[base], sc.at[base + 1 + i], peer) for i, peer in enumerate(peers)],
                        sc.at[pl.ds(base + 1, len(peers))])

    def collect(key, base, peers):
        got[key].wait_recv()
        v = sc[base]
        for i in range(len(peers)):
            v = v + sc[base + 1 + i]
        return v

    keep = {}
    @task("v1")
    def _():
        owners()
        direct = lax.dot_general(sv3[...], x[0, pl.ds(0, 2)].reshape(half, feats), NT, preferred_element_type=F32)
        direct = jnp.where(lane < rows, direct[0:1] + direct[1:2] + direct[2:3], 0.0)
        cand = lax.broadcasted_iota(jnp.int32, (128, 128), 0).astype(F32)
        per = 128 // rows
        sums = jnp.zeros((16, 128), F32)
        for w in range(NW):
            for h in range(2):
                who = jnp.zeros((1, 128), F32)
                for p in range(per):
                    who = jnp.where(lane // rows == p, ow[w, 2 * h + p // NY, p % NY][0:1], who)
                score = rsc[w, :, pl.ds(h * 128, 128)]
                score = score[0:1] + score[1:2] + score[2:3]
                if w == 0 and h == 0:
                    score = score + direct
                terms = stacked(split(score, 3) + [jnp.ones((1, 128), BF)], 16)
                sums = sums + lax.dot_general(terms, jnp.where(cand == who, 1.0, 0.0).astype(BF), NT,
                                              preferred_element_type=F32)
        keep["count"] = sums[3:4]
        exchange("s1", bases[0], sums[0:1] + sums[1:2] + sums[2:3], tp_peers)

    @task("v2")
    def _():
        exchange("s2", bases[1], collect("s1", bases[0], tp_peers), y_peers)

    @task("v3")
    def _():
        exchange("s3", bases[2], collect("s2", bases[1], y_peers), z_peers)

    assert sorted(ORDER) == sorted(tasks)
    early = ("wts", "vec")
    for name in early:
        tasks[name]()
    pl.semaphore_wait(barrier, len(tp_peers + y_peers + z_peers))
    for name in ORDER:
        if name not in early:
            tasks[name]()

    v = fs[0].astype(F32)
    for w in range(1, NW):
        got["rf", w].wait_recv()
        v = v + rf[w - 1].astype(F32)
    out_ref[...] = v
    assert (used[0], len(kinds)) == (rsem.shape[0], ssem.shape[0])
    score_ref[...] = collect("s3", bases[2], z_peers) / keep["count"]
    for copy in flying:
        copy.wait_send()
    later = pl.ds(1, NW - 1)
    every = {
        "far": x.at[later, 0, 0], "p2": x.at[:, 0, pl.ds(1, 3), :, A], "q2": x.at[:, pl.ds(1, 3), 0, :, B],
        "p3": x.at[:, pl.ds(1, 3), :, :, A], "q3": x.at[:, :, pl.ds(1, 3), :, B], "c1": rc, "x": rx,
        "h": hid.at[:, cc, pl.ds(0, NX - 1)], "c2": hid.at[:, cc], "r1p": r1p, "r1q": r1q, "r2p": r2p, "r2q": r2q,
        "rf": rf,
    }
    for kind, union in every.items():
        pltpu.make_async_remote_copy(src_ref=union, dst_ref=union, send_sem=ssem.at[kinds[kind]], recv_sem=rsem.at[0],
                                     device_id=tp_peers[0], device_id_type=MESH).wait_send()


def shards(preview, row_owner, norm_gain, w_gate, w_up, w_down, score_vec):
    rows, feats = preview.shape
    hidden = w_gate.shape[0]
    hpad = -(-hidden // 128) * 128
    half, blk, wide = 2 * NY * rows, 2 * NY * rows // NX, 2 * hidden
    pa = feats // 256 * 128
    pb = feats - pa
    sems, kinds = 61, 21
    vmem = pl.BlockSpec(memory_space=pltpu.VMEM)
    hbm = pl.BlockSpec(memory_space=pl.ANY)
    verified, scores = pl.pallas_call(
        functools.partial(kernel, pa),
        out_shape=(jax.ShapeDtypeStruct((rows, feats), F32), jax.ShapeDtypeStruct((1, 128), F32)),
        in_specs=[hbm, pl.BlockSpec(memory_space=pltpu.SMEM), hbm, hbm, hbm, hbm, hbm],
        out_specs=(vmem, vmem),
        scratch_shapes=[
            pltpu.VMEM((rows, feats), BF),
            pltpu.VMEM((1, feats), F32),
            pltpu.VMEM((1, feats), F32),
            pltpu.VMEM((NW, 4, NY, rows, feats), BF),
            pltpu.VMEM((2 * hidden, feats), BF),
            pltpu.VMEM((feats, 2 * hidden), BF),
            pltpu.VMEM((hpad, feats), BF),
            pltpu.VMEM((16, hpad), BF),
            pltpu.VMEM((16, feats), BF),
            pltpu.VMEM((2 * NX, 1, 128), F32),
            pltpu.VMEM((NW, half, wide), BF),
            pltpu.VMEM((NW, NX, blk, wide), F32),
            pltpu.VMEM((NW, NX, blk, wide), BF),
            pltpu.VMEM((NW, half, wide), BF),
            pltpu.VMEM((NW, NX - 1, blk, wide), BF),
            pltpu.VMEM((NW, 2, NX, blk, hpad), BF),
            pltpu.VMEM((NW, 4, NY, rows, feats), BF),
            pltpu.VMEM((NW, 3, NY, rows, pa), BF),
            pltpu.VMEM((NW, 3, 4, rows, pb), BF),
            pltpu.VMEM((NW, 3, rows, pa), BF),
            pltpu.VMEM((NW, 3, rows, pb), BF),
            pltpu.VMEM((NW, rows, feats), BF),
            pltpu.VMEM((NW - 1, rows, feats), BF),
            pltpu.VMEM((NW, 4, NY, 2, 128), F32),
            pltpu.VMEM((NW, 8, 2 * half), F32),
            pltpu.VMEM((2 * NX + NY + NZ, 1, 128), F32),
            pltpu.SemaphoreType.DMA((8,)),
            pltpu.SemaphoreType.DMA((kinds,)),
            pltpu.SemaphoreType.DMA((sems,)),
        ],
        compiler_params=pltpu.CompilerParams(
            collective_id=0, has_side_effects=True, vmem_limit_bytes=56 << 20),
    )(preview, row_owner, norm_gain[None, :], w_gate, w_up, w_down, score_vec[None, :])
    return (verified + preview.astype(F32)).astype(BF), scores[0, :CAND]


def solution(mesh):
    placed = (
        P("section", "tp"),
        P("section"),
        P("tp"),
        P("section", "tp"),
        P("section", "tp"),
        P("section", "tp"),
        P("tp"),
    )
    return jax.shard_map(
        shards, mesh=mesh, in_specs=placed, out_specs=(P("section", "tp"), P()), check_vma=False
    )
```
